128 devices in a mesh: px: 8 (over x, core), py: 16 (over z, y).
Axes of the slice: x: 4, y: 4, z: 4, core: 2. Of those that a mesh axis runs over, the one named last changes fastest.
Arguments:
- theta: float32 [58, 128, 4096], P(None, 'px', 'py'), may hold values from 0.5 to 1.5
- vapor: float32 [58, 128, 4096], P(None, 'px', 'py'), may hold values from 0.1 to 1
- cloud: float32 [58, 128, 4096], P(None, 'px', 'py'), may hold values from 0 to 0.4
- divergence: float32 [58, 128, 4096], P(None, 'px', 'py'), may hold values from -6 to 6
- edge_weight: float32 [3, 128, 4096], P(None, 'px', 'py'), may hold values from 0.5 to 2
- inv_area: float32 [128, 4096], P('px', 'py'), may hold values from 0.7 to 1.4
- damping: float32 [3, 58], replicated, may hold values from 0.0005 to 0.004
- exner: float32 [58], replicated, may hold values from 0.6 to 1
- sat_scale: float32 [58], replicated, may hold values from 0.1 to 0.6
- layer_mass: float32 [58], replicated, may hold values from 0.02 to 0.1
- span_of: int32 [128, 4096], P('px', 'py'), may hold values from 0 to 65535, as said below
Outputs:
- theta_next: float32 [58, 128, 4096], P(None, 'px', 'py')
- vapor_next: float32 [58, 128, 4096], P(None, 'px', 'py')
- cloud_next: float32 [58, 128, 4096], P(None, 'px', 'py')
- divergence_next: float32 [58, 128, 4096], P(None, 'px', 'py')
- precip_spans: float32 [8, 65536], P('px', 'py')
The draws below stay inside these ranges and needn't reach their ends.
Inputs may be any that keep to these rules, and one draw needn't show every extreme that they name: `span_of`: position p of px index a belongs to device p // 4096 of the py row of a. Within the 16 rows of one px index the entries are a permutation. The columns of one device take exactly 192 positions of every device of its row and 1024 more positions of one other device of that row, so each device receives exactly 4096 positions.
All inputs are finite; a program needn't handle non-finite values.
Results may differ from the reference program's by a relative error of at most 0.00002.
Values sent between devices are 32-bit elements; how exact they have to be, the bound alone decides.
No kernel may reach another device: no remote copies, remote signals or barrier semaphores. Data moves between devices by JAX's collectives and lax.ppermute only.
A program may use at most 128 MiB of HBM per device.

```python
import math
import jax
import jax.numpy as jnp

L = 58
CX = 16
CY = 256
NSAT = 2
NX = 128
NY = 4096
N_PX = 8
N_PY = 16


def row_positions(row_key):
    peers = N_PY
    column_total = CX * CY
    quarter = column_total // 4
    group_size = 3 * column_total // (4 * peers)
    partner_shift = jax.random.randint(jax.random.fold_in(row_key, 1), (), 1, peers)
    source_orders = jax.vmap(lambda sub_key: jax.random.permutation(sub_key, column_total))(jax.random.split(jax.random.fold_in(row_key, 2), peers))
    target_orders = jax.vmap(lambda sub_key: jax.random.permutation(sub_key, column_total))(jax.random.split(jax.random.fold_in(row_key, 3), peers))
    places = jnp.arange(column_total, dtype=jnp.int32)[None, :]
    sources = jnp.arange(peers, dtype=jnp.int32)[:, None]
    in_group = places >= quarter
    target = jnp.where(in_group, (places - quarter) // group_size, (sources + partner_shift) % peers)
    arrival = jnp.where(in_group, sources * group_size + (places - quarter) % group_size, peers * group_size + places)
    placed = target * column_total + jnp.take(target_orders.reshape(-1), target * column_total + arrival)
    result = jnp.zeros((peers, column_total), jnp.int32).at[sources, source_orders].set(placed.astype(jnp.int32))
    return result


def draw_span_of(key, part):
    row_keys = jax.random.split(jax.random.fold_in(key, 7), N_PX)
    blocks = jax.vmap(row_positions)(row_keys)
    blocks = blocks.reshape(N_PX, N_PY, CX, CY).transpose(0, 2, 1, 3)
    return blocks.reshape(NX, NY).astype(jnp.int32)


def block_levels(rng, dims, shards, low, high):
    def one(position, parts):
        draws = jax.random.uniform(jax.random.fold_in(jax.random.fold_in(rng, 6), position), (parts,), jnp.float32, low / len(shards), high / len(shards))
        return jnp.repeat(jnp.exp(draws), dims[position] // parts).reshape((-1,) + (1,) * (len(dims) - position - 1))

    loudness = one(*shards[0])
    for cut in shards[1:]:
        loudness = loudness * one(*cut)
    return loudness


def bell_draw(own_key, dims, width, limit, cuts=(), held_as=jnp.bfloat16):
    drawn = jax.random.normal(own_key, dims, jnp.float32) * width
    if len(cuts) > 0:
        drawn = block_levels(own_key, dims, cuts, -0.22, 0.18) * drawn
    return jnp.clip(drawn, min=-limit, max=limit).astype(held_as)


def setup_inputs(seed: int = 0) -> dict:
    seeds = jax.random.split(jax.random.key(seed), 12)
    theta = jnp.clip(0.5 + 1.0 * jax.random.uniform(seeds[0], (L, NX, NY), jnp.float32) ** block_levels(seeds[0], (L, NX, NY), ((1, 8), (2, 16)), -0.2, 0.2), 0.5, 1.5)
    vapor = jnp.clip(0.1 + 0.9 * jax.random.uniform(seeds[1], (L, NX, NY), jnp.float32) ** block_levels(seeds[1], (L, NX, NY), ((1, 8), (2, 16)), -0.2, 0.2), 0.1, 1.0)
    cloud = jnp.clip(0.4 * jax.random.uniform(seeds[2], (L, NX, NY), jnp.float32) ** block_levels(seeds[2], (L, NX, NY), ((1, 8), (2, 16)), -0.2, 0.2), 0.0, 0.4)
    divergence = bell_draw(seeds[3], (L, NX, NY), 1.0, 6.0, ((1, 8), (2, 16)), jnp.float32)
    edge_weight = jnp.clip(jnp.exp(math.log(2.0) - 1.3862944 * jax.random.uniform(seeds[4], (3, NX, NY), jnp.float32) ** block_levels(seeds[4], (3, NX, NY), ((1, 8), (2, 16)), -0.2, 0.2)), 0.5, 2.0)
    inv_area = jnp.clip(jnp.exp(math.log(1.4) - 0.6931472 * jax.random.uniform(seeds[5], (NX, NY), jnp.float32) ** block_levels(seeds[5], (NX, NY), ((0, 8), (1, 16)), -0.2, 0.2)), 0.7, 1.4)
    damping = jnp.clip(jnp.exp(jax.random.uniform(seeds[6], (3, L), jnp.float32, math.log(0.0005), math.log(0.004))), 0.0005, 0.004)
    exner = jnp.clip(jnp.exp(jax.random.uniform(seeds[7], (L,), jnp.float32, math.log(0.6), math.log(1.0))), 0.6, 1.0)
    sat_scale = jnp.clip(jnp.exp(jax.random.uniform(seeds[8], (L,), jnp.float32, math.log(0.1), math.log(0.6))), 0.1, 0.6)
    layer_mass = jnp.clip(jnp.exp(jax.random.uniform(seeds[9], (L,), jnp.float32, math.log(0.02), math.log(0.1))), 0.02, 0.1)
    span_of = draw_span_of(jax.random.fold_in(seeds[11], 71), 0)
    return {"theta": theta, "vapor": vapor, "cloud": cloud, "divergence": divergence, "edge_weight": edge_weight, "inv_area": inv_area, "damping": damping, "exner": exner, "sat_scale": sat_scale, "layer_mass": layer_mass, "span_of": span_of}


LATENT = 0.5
QCRIT = 0.2
AUTO_RATE = 0.5


def shifted(array_in, step_row, step_col):
    height = array_in.shape[-2]
    breadth = array_in.shape[-1]
    return array_in[..., 1 + step_row:height - 1 + step_row, 1 + step_col:breadth - 1 + step_col]


def laplace(values, weights, inverse):
    centre = shifted(values, 0, 0)
    summed = shifted(weights[0], 0, 0) * (shifted(values, 1, 0) - centre)
    summed = summed + shifted(weights[0], -1, 0) * (shifted(values, -1, 0) - centre)
    summed = summed + shifted(weights[1], 0, 0) * (shifted(values, 0, 1) - centre)
    summed = summed + shifted(weights[1], 0, -1) * (shifted(values, 0, -1) - centre)
    summed = summed + shifted(weights[2], 0, 0) * (shifted(values, -1, 1) - centre)
    summed = summed + shifted(weights[2], 1, -1) * (shifted(values, 1, -1) - centre)
    return shifted(inverse, 0, 0) * summed


def adjust(theta_dyn, vapor_dyn, cloud, exner, sat_scale, layer_mass):
    temper = theta_dyn * exner
    condensed = jnp.zeros_like(theta_dyn)
    for repeat in range(NSAT):
        warmed = temper + LATENT * condensed
        saturation = sat_scale * jnp.exp(warmed)
        excess = vapor_dyn - condensed - saturation
        slope = -1.0 - LATENT * saturation
        condensed = condensed - excess / slope
    condensed = jnp.maximum(condensed, -cloud)
    theta_next = theta_dyn + LATENT * condensed / exner
    vapor_next = vapor_dyn - condensed
    liquid = cloud + condensed
    rained = AUTO_RATE * jnp.maximum(liquid - QCRIT, 0.0)
    cloud_next = liquid - rained
    precip = jnp.sum(layer_mass * rained, axis=0)
    return theta_next, vapor_next, cloud_next, precip


def reference(theta, vapor, cloud, divergence, edge_weight, inv_area, damping, exner, sat_scale, layer_mass, span_of):
    fields = jnp.concatenate([theta, vapor, divergence], 0)
    geometry = jnp.concatenate([edge_weight, inv_area[None]], 0)
    padded = jnp.pad(fields, ((0, 0), (2, 2), (2, 2)), mode="wrap")
    geometry_pad = jnp.pad(geometry, ((0, 0), (2, 2), (2, 2)), mode="wrap")
    lap_once = laplace(padded, geometry_pad[:3], geometry_pad[3])
    inner_geo = geometry_pad[:, 1:-1, 1:-1]
    second = laplace(lap_once, inner_geo[:3], inner_geo[3])
    damped = fields - damping.reshape(3 * L)[:, None, None] * second
    theta_next, vapor_next, cloud_next, precip = adjust(
        damped[:L], damped[L:2 * L], cloud,
        exner[:, None, None], sat_scale[:, None, None], layer_mass[:, None, None])
    divergence_next = damped[2 * L:]
    rain_rows = precip.reshape(N_PX, CX * NY)
    place_rows = span_of.reshape(N_PX, CX * NY)

    def place_row(places, rainfall):
        return jnp.zeros((CX * NY,), jnp.float32).at[places].set(rainfall)

    precip_spans = jax.vmap(place_row)(place_rows, rain_rows)
    return theta_next, vapor_next, cloud_next, divergence_next, precip_spans
```

```python
import functools

import jax
import jax.numpy as jnp
from jax import lax
from jax.experimental import pallas as pl
from jax.experimental.pallas import tpu as pltpu
from jax.sharding import PartitionSpec as P

LATENT = 0.5
QCRIT = 0.2
AUTO_RATE = 0.5

LANES = 128
BLOCK_LEVELS = 15


def pack_kernel(theta_ref, vapor_ref, div_ref, edge_ref, inv_ref, top_ref, bot_ref, left_ref, right_ref):
    levels = theta_ref.shape[0] // 16
    total = 3 * levels + 4
    fields = (theta_ref, vapor_ref, div_ref)
    for out_ref, first in ((top_ref, 0), (bot_ref, 14)):
        for row in range(2):
            for g in range(3):
                out_ref[pl.ds(row * total + 3 * levels + g, 1), :] = edge_ref[
                    pl.ds(16 * g + first + row, 1), :
                ]
            out_ref[pl.ds(row * total + 3 * levels + 3, 1), :] = inv_ref[pl.ds(first + row, 1), :]
    lane = lax.broadcasted_iota(jnp.int32, (16, LANES), 1)

    def place(acc, value, slot, side):
        shift = 2 * slot if side == 0 else 2 * slot + 2
        moved = pltpu.roll(value, lax.rem(shift, LANES), 1)
        return jnp.where((lane >> 1) == slot, moved, acc)

    def body(l, accs):
        out = []
        for field, ref in enumerate(fields):
            base = pl.multiple_of(l * 16, 16)
            for row in range(2):
                at = pl.ds(row * total + field * levels + l, 1)
                top_ref[at, :] = ref[pl.ds(base + row, 1), :]
                bot_ref[at, :] = ref[pl.ds(base + 14 + row, 1), :]
            for side in range(2):
                value = ref[pl.ds(base, 16), side * LANES : (side + 1) * LANES]
                out.append(place(accs[2 * field + side], value, l, side))
        return tuple(out)

    zero = jnp.zeros((16, LANES), jnp.float32)
    accs = list(lax.fori_loop(0, levels, body, (zero,) * 6))
    for g in range(4):
        for side in range(2):
            cols = slice(side * LANES, (side + 1) * LANES)
            value = edge_ref[16 * g : 16 * g + 16, cols] if g < 3 else inv_ref[:, cols]
            accs[side] = place(accs[side], value, jnp.int32(levels + g), side)
    for field in range(3):
        left_ref[:, field * LANES : (field + 1) * LANES] = accs[2 * field]
        right_ref[:, field * LANES : (field + 1) * LANES] = accs[2 * field + 1]


def pack(theta, vapor, divergence, edge, inv):
    levels = theta.shape[0] // 16
    total = 3 * levels + 4
    rows = jax.ShapeDtypeStruct((2 * total, 256), jnp.float32)
    cols = jax.ShapeDtypeStruct((16, 3 * LANES), jnp.float32)
    return pl.pallas_call(
        pack_kernel,
        out_shape=(rows, rows, cols, cols),
        name="pack",
    )(theta, vapor, divergence, edge, inv)


def up(v):
    return pltpu.roll(v, v.shape[0] - 1, 0)


def down(v):
    return pltpu.roll(v, 1, 0)


def ahead(v):
    return pltpu.roll(v, v.shape[1] - 1, 1)


def behind(v):
    return pltpu.roll(v, 1, 1)


def main_kernel(
    peers,
    levels,
    params_ref,
    theta_ref,
    vapor_ref,
    cloud_ref,
    div_ref,
    edge_ref,
    inv_ref,
    span_ref,
    below_ref,
    above_ref,
    colr_ref,
    coll_ref,
    corner_below_ref,
    corner_above_ref,
    theta_out,
    vapor_out,
    cloud_out,
    div_out,
    send_out,
    coef_ref,
    rain_ref,
    hi_ref,
    lo_ref,
):
    total = 3 * levels + 4
    step = pl.program_id(0)
    steps = pl.num_programs(0)

    lane = lax.broadcasted_iota(jnp.int32, (8, LANES), 1)
    sub = lax.broadcasted_iota(jnp.int32, (8, 256), 0)
    sub_c = lax.broadcasted_iota(jnp.int32, (8, LANES), 0)
    lane16 = lax.broadcasted_iota(jnp.int32, (16, LANES), 1)

    def side_tile(field, slot):
        cols = slice(field * LANES, (field + 1) * LANES)
        to_right = lax.rem(LANES - 2 * slot, LANES)
        to_left = lax.rem(2 * LANES - 2 - 2 * slot, LANES)
        right = pltpu.roll(colr_ref[:, cols], to_right, 1)
        left = pltpu.roll(coll_ref[:, cols], to_left, 1)
        tile = jnp.where(lane16 < 64, right, left)
        wide = slice((3 + field) * LANES, (4 + field) * LANES)
        corner_r = jnp.where(sub_c < 4, corner_below_ref[:, cols], corner_above_ref[:, cols])
        corner_l = jnp.where(sub_c < 4, corner_below_ref[:, wide], corner_above_ref[:, wide])
        corner = jnp.where(
            lane < 64, pltpu.roll(corner_r, to_right, 1), pltpu.roll(corner_l, to_left, 1)
        )
        return tile, corner

    def row_tile(index):
        def row(ref, r):
            return jnp.broadcast_to(ref[pl.ds(r * total + index, 1), :], (8, 256))

        low = jnp.where(sub < 1, row(below_ref, 0), row(below_ref, 1))
        high = jnp.where(sub < 7, row(above_ref, 0), row(above_ref, 1))
        return jnp.where(sub < 4, low, high)

    def extend(centre, index, field, slot):
        tile, corner = side_tile(field, slot)
        upper = jnp.concatenate([centre, tile], axis=1)
        lower = jnp.concatenate([row_tile(index), corner], axis=1)
        return jnp.concatenate([upper, lower], axis=0)

    @pl.when(step == 0)
    def _():
        geo = []
        for g in range(4):
            centre = edge_ref[16 * g : 16 * g + 16, :] if g < 3 else inv_ref[...]
            geo.append(extend(centre, 3 * levels + g, 0, jnp.int32(levels + g)))
        w0, w1, w2, inv = geo
        c1 = inv * w0
        c2 = inv * down(w0)
        c3 = inv * w1
        c4 = inv * behind(w1)
        c5 = inv * w2
        c6 = inv * behind(up(w2))
        coef_ref[0] = c1 + c2 + c3 + c4 + c5 + c6
        coef_ref[1] = c1
        coef_ref[2] = c2
        coef_ref[3] = behind(c3)
        coef_ref[4] = ahead(c4)
        coef_ref[5] = behind(c5)
        coef_ref[6] = ahead(c6)
        rain_ref[...] = jnp.zeros_like(rain_ref)

    def lap(v, high, wide):
        v_up = up(v)[:high]
        v_dn = down(v)[:high]
        v = v[:high]
        a = coef_ref[3, :high] * v + coef_ref[5, :high] * v_dn
        b = coef_ref[4, :high] * v + coef_ref[6, :high] * v_up
        a = ahead(a)[:, :wide]
        b = behind(b)[:, :wide]
        c = (
            coef_ref[1, :high, :wide] * v_up[:, :wide]
            + coef_ref[2, :high, :wide] * v_dn[:, :wide]
            - coef_ref[0, :high, :wide] * v[:, :wide]
        )
        return (a + b) + c

    def damp(centre, field, l):
        first = lap(extend(centre, field * levels + l, field, l), 24, 384)
        second = lap(first, 16, 256)
        return centre - params_ref[field * levels + l] * second

    def body(k, carry):
        l = step * BLOCK_LEVELS + k
        div_out[k] = damp(div_ref[k], 2, l)
        theta = damp(theta_ref[k], 0, l)
        vapor = damp(vapor_ref[k], 1, l)
        exner = params_ref[3 * levels + l]
        scale = params_ref[4 * levels + l]
        mass = params_ref[5 * levels + l]
        cloud = cloud_ref[k]
        temper = theta * exner
        saturation = scale * jnp.exp(temper)
        condensed = (vapor - saturation) / (1.0 + LATENT * saturation)
        saturation = scale * jnp.exp(temper + LATENT * condensed)
        condensed = condensed + (vapor - condensed - saturation) / (1.0 + LATENT * saturation)
        condensed = jnp.maximum(condensed, -cloud)
        ratio = jnp.full((1, 256), LATENT, jnp.float32) / jnp.full((1, 256), exner, jnp.float32)
        theta_out[k] = theta + condensed * ratio
        vapor_out[k] = vapor - condensed
        liquid = cloud + condensed
        rained = AUTO_RATE * jnp.maximum(liquid - QCRIT, 0.0)
        cloud_out[k] = liquid - rained
        rain_ref[...] += mass * rained
        return carry

    lax.fori_loop(0, jnp.minimum(BLOCK_LEVELS, levels - step * BLOCK_LEVELS), body, 0)

    @pl.when(step == steps - 1)
    def _():
        tall = lax.broadcasted_iota(jnp.int32, (peers * 32, 256), 0)
        short = lax.broadcasted_iota(jnp.int32, (LANES, 256), 0)
        for r in range(16):
            span = span_ref[r : r + 1, :]
            value = rain_ref[r : r + 1, :]
            coarse = value.astype(jnp.bfloat16).astype(jnp.float32)
            fine = value - coarse
            cols = slice(r * 256, (r + 1) * 256)
            hi_ref[:, cols] = jnp.where(tall == (span >> 7), 1.0, 0.0).astype(jnp.bfloat16)
            here = short == (span & 127)
            lo_ref[:LANES, cols] = jnp.where(here, coarse, 0.0).astype(jnp.bfloat16)
            lo_ref[LANES:, cols] = jnp.where(here, fine, 0.0).astype(jnp.bfloat16)
        placed = lax.dot_general(
            hi_ref[...], lo_ref[...], (((1,), (1,)), ((), ())), preferred_element_type=jnp.float32
        )
        send_out[...] = placed[:, :LANES] + placed[:, LANES:]


def physics(peers, params, theta, vapor, cloud, divergence, edge, inv, span, halos):
    levels = theta.shape[0]
    steps = pl.cdiv(levels, BLOCK_LEVELS)
    block = pl.BlockSpec((BLOCK_LEVELS, 16, 256), lambda s: (s, 0, 0))
    whole = lambda a: pl.BlockSpec(a.shape, lambda s: (0,) * a.ndim)
    field = jax.ShapeDtypeStruct(theta.shape, jnp.float32)
    sent = jax.ShapeDtypeStruct((peers * 32, LANES), jnp.float32)
    return pl.pallas_call(
        functools.partial(main_kernel, peers, levels),
        grid=(steps,),
        in_specs=[pl.BlockSpec(memory_space=pltpu.SMEM), block, block, block, block]
        + [whole(a) for a in (edge, inv, span) + halos],
        out_specs=[block, block, block, block, whole(sent)],
        out_shape=[field, field, field, field, sent],
        scratch_shapes=[
            pltpu.VMEM((7, 24, 384), jnp.float32),
            pltpu.VMEM((16, 256), jnp.float32),
            pltpu.VMEM((peers * 32, 4096), jnp.bfloat16),
            pltpu.VMEM((2 * LANES, 4096), jnp.bfloat16),
        ],
        name="physics",
    )(params, theta, vapor, cloud, divergence, edge, inv, span, *halos)


def on_device(
    theta,
    vapor,
    cloud,
    divergence,
    edge_weight,
    inv_area,
    damping,
    exner,
    sat_scale,
    layer_mass,
    span_of,
):
    levels = theta.shape[0]
    n_px = lax.axis_size("px")
    peers = lax.axis_size("py")

    def from_next(x, axis, count):
        return lax.ppermute(x, axis, [((i + 1) % count, i) for i in range(count)])

    def from_prev(x, axis, count):
        return lax.ppermute(x, axis, [(i, (i + 1) % count) for i in range(count)])

    flat = lambda x: x.reshape(-1, 256)
    edge = flat(edge_weight)
    top, bot, left, right = pack(flat(theta), flat(vapor), flat(divergence), edge, inv_area)
    colr = from_next(left, "py", peers)
    coll = from_prev(right, "py", peers)
    below = from_next(top, "px", n_px)
    above = from_prev(bot, "px", n_px)
    sides = jnp.concatenate([colr, coll], axis=1)
    corner_below = from_next(sides[:8], "px", n_px)
    corner_above = from_prev(sides[8:], "px", n_px)
    params = jnp.concatenate([damping.reshape(-1), exner, sat_scale, layer_mass])
    theta_next, vapor_next, cloud_next, divergence_next, send = physics(
        peers,
        params,
        theta,
        vapor,
        cloud,
        divergence,
        edge,
        inv_area,
        span_of,
        (below, above, colr, coll, corner_below, corner_above),
    )
    got = lax.all_to_all(send.reshape(peers, 32, LANES), "py", split_axis=0, concat_axis=0, tiled=True)
    precip = jnp.sum(got, axis=0).reshape(1, 4096)
    return (theta_next, vapor_next, cloud_next, divergence_next, precip)


def solution(mesh):
    field = P(None, "px", "py")
    plane = P("px", "py")
    return jax.shard_map(
        on_device,
        mesh=mesh,
        in_specs=(field, field, field, field, field, plane, P(), P(), P(), P(), plane),
        out_specs=(field, field, field, field, plane),
        check_vma=False,
    )
```

```python
import functools

import jax
import jax.numpy as jnp
from jax import lax
from jax.experimental import pallas as pl
from jax.experimental.pallas import tpu as pltpu
from jax.sharding import PartitionSpec as P

LATENT = 0.5
QCRIT = 0.2
AUTO_RATE = 0.5

LANES = 128
BLOCK_LEVELS = 16
UNROLL = 2


def pack_kernel(
    theta0, theta1, vapor0, vapor1, div0, div1, edge_ref, inv_ref,
    top_ref, bot_ref, left_ref, right_ref, left_low, left_high, right_low, right_high,
):
    levels = theta0.shape[0] // 16
    total = 3 * levels + 4
    fields = ((theta0, theta1), (vapor0, vapor1), (div0, div1))
    for out_ref, first in ((top_ref, 0), (bot_ref, 14)):
        for row in range(2):
            for field, halves in enumerate(fields):
                at = pl.ds(row * total + field * levels, levels)
                for half, ref in enumerate(halves):
                    cols = slice(half * LANES, (half + 1) * LANES)
                    out_ref[at, cols] = ref[pl.ds(first + row, levels, stride=16), :]
            for g in range(3):
                out_ref[pl.ds(row * total + 3 * levels + g, 1), :] = edge_ref[
                    pl.ds(16 * g + first + row, 1), :
                ]
            out_ref[pl.ds(row * total + 3 * levels + 3, 1), :] = inv_ref[pl.ds(first + row, 1), :]
    pair = lax.broadcasted_iota(jnp.int32, (16, LANES), 1) >> 1
    low_base = 2 * total + 4

    def place(acc, value, slot, side):
        moved = pltpu.roll(value, (2 * slot + 2 * side) % LANES, 1)
        return jnp.where(pair == slot, moved, acc)

    for field, halves in enumerate(fields):
        for side in range(2):
            acc = jnp.zeros((16, LANES), jnp.float32)
            for l in range(levels):
                acc = place(acc, halves[side][16 * l : 16 * l + 16, :], l, side)
            if field == 0:
                cols = slice(side * LANES, (side + 1) * LANES)
                for g in range(4):
                    value = edge_ref[16 * g : 16 * g + 16, cols] if g < 3 else inv_ref[:, cols]
                    acc = place(acc, value, levels + g, side)
            cols = slice(field * LANES, (field + 1) * LANES)
            whole, low, high = (
                (left_ref, left_low, left_high) if side == 0 else (right_ref, right_low, right_high)
            )
            whole[:, cols] = acc
            low[:, cols] = acc[:8]
            high[:, cols] = acc[8:]
            slot = 3 * side + field
            rows = pl.ds(low_base + 8 * (slot // 2), 8)
            cols = slice((slot % 2) * LANES, (slot % 2 + 1) * LANES)
            top_ref[rows, cols] = acc[:8]
            bot_ref[rows, cols] = acc[8:]


def pack(theta, vapor, divergence, edge, inv):
    levels = theta.shape[0] // 16
    total = 3 * levels + 4
    rows = jax.ShapeDtypeStruct((2 * total + 28, 256), jnp.float32)
    cols = jax.ShapeDtypeStruct((16, 3 * LANES), jnp.float32)
    half = jax.ShapeDtypeStruct((8, 3 * LANES), jnp.float32)
    sides = [pl.BlockSpec((16 * levels, LANES), lambda s, c=c: (0, c)) for c in range(2)]
    whole = lambda a: pl.BlockSpec(a.shape, lambda s: (0,) * len(a.shape))
    outs = (rows, rows, cols, cols, half, half, half, half)
    return pl.pallas_call(
        pack_kernel,
        grid=(1,),
        in_specs=sides * 3 + [whole(edge), whole(inv)],
        out_specs=[whole(o) for o in outs],
        out_shape=outs,
        name="pack",
    )(theta, theta, vapor, vapor, divergence, divergence, edge, inv)


def onehot_kernel(high, span_ref, out_ref):
    def count(rows, shift):
        index = lax.broadcasted_iota(jnp.int32, (rows, 256), 0) - shift
        return index.astype(jnp.float32).astype(jnp.bfloat16)

    tall = count(high, high // 2)
    short = count(LANES, 0)
    one = jnp.bfloat16(1.0)
    zero = jnp.bfloat16(0.0)
    for r in range(span_ref.shape[0]):
        span = span_ref[r : r + 1, :]
        hi = ((span >> 7) - high // 2).astype(jnp.float32).astype(jnp.bfloat16)
        lo = (span & 127).astype(jnp.float32).astype(jnp.bfloat16)
        cols = slice(r * 256, (r + 1) * 256)
        out_ref[:high, cols] = jnp.where(tall == hi, one, zero)
        out_ref[high:, cols] = jnp.where(short == lo, one, zero)


def onehot(span, high):
    shape = jax.ShapeDtypeStruct((high + LANES, 4096), jnp.bfloat16)
    return pl.pallas_call(
        functools.partial(onehot_kernel, high),
        grid=(2,),
        in_specs=[pl.BlockSpec((8, 256), lambda s: (s, 0))],
        out_specs=pl.BlockSpec((high + LANES, 2048), lambda s: (0, s)),
        out_shape=shape,
        name="onehot",
        cost_estimate=pl.CostEstimate(flops=10**9, transcendentals=0, bytes_accessed=5 * 2**20),
    )(span)


def up(v):
    return pltpu.roll(v, v.shape[0] - 1, 0)


def down(v):
    return pltpu.roll(v, 1, 0)


def ahead(v):
    return pltpu.roll(v, v.shape[1] - 1, 1)


def behind(v):
    return pltpu.roll(v, 1, 1)


def main_kernel(
    peers, levels,
    damping_ref, exner_ref, scale_ref, mass_ref,
    theta_ref, vapor_ref, cloud_ref, div_ref, edge_ref, inv_ref, onehot_hbm,
    below_ref, above_ref, colr_ref, coll_ref, ownl_ref, ownr_ref,
    diag_br, diag_ar, diag_bl, diag_al,
    theta_out, vapor_out, cloud_out, div_out, send_out,
    coef_ref, edge_a, edge_b, rain_ref, onehot_ref, lo_ref, sem,
):
    total = 3 * levels + 4
    high = peers * 32
    step = pl.program_id(0)
    steps = pl.num_programs(0)
    fetch = pltpu.make_async_copy(onehot_hbm, onehot_ref, sem)

    sub = lax.broadcasted_iota(jnp.int32, (8, 256), 0)
    sub_half = sub[:, :LANES]

    def row_tile(index):
        def row(ref, r):
            return jnp.broadcast_to(ref[pl.ds(r * total + index, 1), :], (8, 256))

        low = jnp.where(sub < 1, row(below_ref, 0), row(below_ref, 1))
        top = jnp.where(sub < 7, row(above_ref, 0), row(above_ref, 1))
        tile = jnp.where(sub < 4, low, top)
        return tile[:, :LANES], tile[:, LANES:]

    @pl.when(step == 0)
    def _():
        fetch.start()
        lane24 = lax.broadcasted_iota(jnp.int32, (24, LANES), 1)
        even = (lane24 & 1) == 0

        def packed(own, low, top, cols):
            corner = jnp.where(sub_half < 4, low, top)
            return jnp.concatenate([own[:, cols], corner], axis=0)

        def side_packs(field):
            cols = slice(field * LANES, (field + 1) * LANES)

            def inner(ref, slot):
                rows = pl.ds(2 * total + 4 + 8 * (slot // 2), 8)
                return ref[rows, (slot % 2) * LANES : (slot % 2 + 1) * LANES]

            v_r = packed(colr_ref, diag_br[:, cols], diag_ar[:, cols], cols)
            v_l = packed(coll_ref, diag_bl[:, cols], diag_al[:, cols], cols)
            o_l = packed(ownl_ref, inner(below_ref, field), inner(above_ref, field), cols)
            o_r = packed(ownr_ref, inner(below_ref, 3 + field), inner(above_ref, 3 + field), cols)
            return v_r, v_l, o_l, o_r

        packs = [side_packs(field) for field in range(3)]
        geo = []
        for g in range(4):
            slot = levels + g
            right = pltpu.roll(packs[0][0], (LANES - 2 * slot) % LANES, 1)
            left = pltpu.roll(packs[0][1], (2 * LANES - 2 - 2 * slot) % LANES, 1)
            side = jnp.where(lane24 < 64, right, left)
            centre = edge_ref[16 * g : 16 * g + 16, :] if g < 3 else inv_ref[...]
            tiles = row_tile(3 * levels + g)
            halves = [
                jnp.concatenate([centre[:, h * LANES : (h + 1) * LANES], tiles[h]], axis=0)
                for h in range(2)
            ]
            geo.append(jnp.concatenate(halves + [side], axis=1))
        w0, w1, w2, inv = geo
        c1 = inv * w0
        c2 = inv * down(w0)
        c3 = inv * w1
        c4 = inv * behind(w1)
        c5 = inv * w2
        c6 = inv * behind(up(w2))
        c0 = c1 + c2 + c3 + c4 + c5 + c6
        shifted = (c0, c1, c2, behind(c3), ahead(c4), behind(c5), ahead(c6))
        for k, c in enumerate(shifted):
            coef_ref[k] = c[:, :256]
        rain_ref[...] = jnp.zeros_like(rain_ref)

        def pick(c, col):
            return jnp.broadcast_to(c[:, col : col + 1], (24, LANES))

        k0, k1, k2, k3, k4, k5, k6 = (
            jnp.where(even, pick(c, 256), pick(c, 383)) for c in (c0, c1, c2, c3, c4, c5, c6)
        )
        x3 = jnp.where(even, pick(c3, 255), pick(c4, 0))
        x5 = jnp.where(even, pick(c5, 255), 0.0)
        x6 = jnp.where(even, 0.0, pick(c6, 0))
        for field in range(3):
            v_r, v_l, o_l, o_r = packs[field]
            v = jnp.where(even, v_r, v_l)
            v_up = up(v)
            v_dn = down(v)
            edge_a[field] = x3 * v + x5 * v_dn + x6 * v_up
            nxt = jnp.where(even, ahead(v_r), behind(o_l))
            prv = jnp.where(even, ahead(o_r), behind(v_l))
            first = (k1 * v_up + k2 * v_dn - k0 * v) + (
                (k3 * nxt + k5 * down(nxt)) + (k4 * prv + k6 * up(prv))
            )
            edge_b[field] = x3 * first + x5 * down(first) + x6 * up(first)

    def lap(halves, edge, rows):
        lane = lax.broadcasted_iota(jnp.int32, (rows, LANES), 1)
        a, b, c = [], [], []
        for h in range(2):
            cols = slice(h * LANES, (h + 1) * LANES)
            v_up = up(halves[h])[:rows]
            v_dn = down(halves[h])[:rows]
            v = halves[h][:rows]
            a.append(ahead(coef_ref[3, :rows, cols] * v + coef_ref[5, :rows, cols] * v_dn))
            b.append(behind(coef_ref[4, :rows, cols] * v + coef_ref[6, :rows, cols] * v_up))
            c.append(
                coef_ref[1, :rows, cols] * v_up
                + coef_ref[2, :rows, cols] * v_dn
                - coef_ref[0, :rows, cols] * v
            )
        last = lane == LANES - 1
        zero = lane == 0
        left = (jnp.where(last, a[1], a[0]) + jnp.where(zero, edge, b[0])) + c[0]
        right = (jnp.where(last, edge, a[1]) + jnp.where(zero, b[0], b[1])) + c[1]
        return left, right

    def damp(ref, k, field, l):
        turn = lax.rem(2 * LANES - 1 - 2 * l, LANES)
        centre = [ref[k, :, h * LANES : (h + 1) * LANES] for h in range(2)]
        tiles = row_tile(field * levels + l)
        first = lap(
            [jnp.concatenate([centre[h], tiles[h]], axis=0) for h in range(2)],
            pltpu.roll(edge_a[field], turn, 1),
            24,
        )
        second = lap(first, pltpu.roll(edge_b[field, :16], turn, 1), 16)
        rate = damping_ref[field, l]
        return [centre[h] - rate * second[h] for h in range(2)]

    def level(k):
        l = step * BLOCK_LEVELS + k
        div = damp(div_ref, k, 2, l)
        thetas = damp(theta_ref, k, 0, l)
        vapors = damp(vapor_ref, k, 1, l)
        exner = exner_ref[l]
        scale = scale_ref[l]
        mass = mass_ref[l]
        ratio = jnp.full((1, LANES), LATENT, jnp.float32) / jnp.full((1, LANES), exner, jnp.float32)
        for h in range(2):
            cols = slice(h * LANES, (h + 1) * LANES)
            theta, vapor = thetas[h], vapors[h]
            div_out[k, :, cols] = div[h]
            cloud = cloud_ref[k, :, cols]
            temper = theta * exner
            saturation = scale * jnp.exp(temper)
            condensed = (vapor - saturation) / (1.0 + LATENT * saturation)
            saturation = scale * jnp.exp(temper + LATENT * condensed)
            condensed = condensed + (vapor - condensed - saturation) / (1.0 + LATENT * saturation)
            condensed = jnp.maximum(condensed, -cloud)
            theta_out[k, :, cols] = theta + condensed * ratio
            vapor_out[k, :, cols] = vapor - condensed
            liquid = cloud + condensed
            rained = AUTO_RATE * jnp.maximum(liquid - QCRIT, 0.0)
            cloud_out[k, :, cols] = liquid - rained
            rain_ref[:, cols] += mass * rained

    def body(m, carry):
        for j in range(UNROLL):
            level(m * UNROLL + j)
        return carry

    count = jnp.minimum(BLOCK_LEVELS, levels - step * BLOCK_LEVELS)
    lax.fori_loop(0, lax.div(count, UNROLL), body, 0)

    @pl.when(step == steps - 1)
    def _():
        fetch.wait()
        for r in range(16):
            value = rain_ref[r : r + 1, :]
            coarse = value.astype(jnp.bfloat16)
            fine = (value - coarse.astype(jnp.float32)).astype(jnp.bfloat16)
            cols = slice(r * 256, (r + 1) * 256)
            here = onehot_ref[high:, cols]
            lo_ref[:LANES, cols] = here * coarse
            lo_ref[LANES:, cols] = here * fine
        placed = lax.dot_general(
            onehot_ref[:high, :],
            lo_ref[...],
            (((1,), (1,)), ((), ())),
            preferred_element_type=jnp.float32,
        )
        send_out[...] = placed[:, :LANES] + placed[:, LANES:]


def physics(peers, scalars, fields, whole_args, marks, halos):
    levels = fields[0].shape[0]
    steps = pl.cdiv(levels, BLOCK_LEVELS)
    high = peers * 32
    block = pl.BlockSpec((BLOCK_LEVELS, 16, 256), lambda s: (s, 0, 0))
    whole = lambda a: pl.BlockSpec(a.shape, lambda s: (0,) * len(a.shape))
    field = jax.ShapeDtypeStruct(fields[0].shape, jnp.float32)
    sent = jax.ShapeDtypeStruct((high, LANES), jnp.float32)
    return pl.pallas_call(
        functools.partial(main_kernel, peers, levels),
        grid=(steps,),
        in_specs=[pl.BlockSpec(memory_space=pltpu.SMEM)] * 4
        + [block] * 4
        + [whole(a) for a in whole_args]
        + [pl.BlockSpec(memory_space=pl.ANY)]
        + [whole(a) for a in halos],
        out_specs=[block, block, block, block, whole(sent)],
        out_shape=[field, field, field, field, sent],
        scratch_shapes=[
            pltpu.VMEM((7, 24, 256), jnp.float32),
            pltpu.VMEM((3, 24, LANES), jnp.float32),
            pltpu.VMEM((3, 24, LANES), jnp.float32),
            pltpu.VMEM((16, 256), jnp.float32),
            pltpu.VMEM((high + LANES, 4096), jnp.bfloat16),
            pltpu.VMEM((2 * LANES, 4096), jnp.bfloat16),
            pltpu.SemaphoreType.DMA(()),
        ],
        name="physics",
    )(*scalars, *fields, *whole_args, marks, *halos)


def on_device(
    theta,
    vapor,
    cloud,
    divergence,
    edge_weight,
    inv_area,
    damping,
    exner,
    sat_scale,
    layer_mass,
    span_of,
):
    n_px = lax.axis_size("px")
    peers = lax.axis_size("py")

    def fetch(x, row, col):
        moves = [
            (((i + row) % n_px) * peers + (j + col) % peers, i * peers + j)
            for i in range(n_px)
            for j in range(peers)
        ]
        return lax.ppermute(x, ("px", "py"), moves)

    flat = lambda x: x.reshape(-1, 256)
    edge = flat(edge_weight)
    top, bot, left, right, left_low, left_high, right_low, right_high = pack(
        flat(theta), flat(vapor), flat(divergence), edge, inv_area
    )
    below = fetch(top, 1, 0)
    above = fetch(bot, -1, 0)
    colr = fetch(left, 0, 1)
    coll = fetch(right, 0, -1)
    diag_br = fetch(left_low, 1, 1)
    diag_ar = fetch(left_high, -1, 1)
    diag_bl = fetch(right_low, 1, -1)
    diag_al = fetch(right_high, -1, -1)
    marks = onehot(span_of, peers * 32)
    theta_next, vapor_next, cloud_next, divergence_next, send = physics(
        peers,
        (damping, exner, sat_scale, layer_mass),
        (theta, vapor, cloud, divergence),
        (edge, inv_area),
        marks,
        (below, above, colr, coll, left, right, diag_br, diag_ar, diag_bl, diag_al),
    )
    got = lax.all_to_all(send.reshape(peers, 32, LANES), "py", split_axis=0, concat_axis=0, tiled=True)
    precip = jnp.sum(got, axis=0).reshape(1, 4096)
    return (theta_next, vapor_next, cloud_next, divergence_next, precip)


def solution(mesh):
    field = P(None, "px", "py")
    plane = P("px", "py")
    return jax.shard_map(
        on_device,
        mesh=mesh,
        in_specs=(field, field, field, field, field, plane, P(), P(), P(), P(), plane),
        out_specs=(field, field, field, field, plane),
        check_vma=False,
    )
```

```python
import functools

import jax
import jax.numpy as jnp
from jax import lax
from jax.experimental import pallas as pl
from jax.experimental.pallas import tpu as pltpu
from jax.sharding import PartitionSpec as P

LATENT = 0.5
QCRIT = 0.2
AUTO_RATE = 0.5

LANES = 128
BLOCK_LEVELS = 16
UNROLL = 2


def pack_kernel(
    theta0, theta1, vapor0, vapor1, div0, div1, edge_ref, inv_ref,
    top_ref, bot_ref, left_ref, right_ref,
):
    levels = theta0.shape[0] // 16
    total = 3 * levels + 4
    fields = ((theta0, theta1), (vapor0, vapor1), (div0, div1))
    for out_ref, first in ((top_ref, 0), (bot_ref, 14)):
        for row in range(2):
            for field, halves in enumerate(fields):
                at = pl.ds(row * total + field * levels, levels)
                for half, ref in enumerate(halves):
                    cols = slice(half * LANES, (half + 1) * LANES)
                    out_ref[at, cols] = ref[pl.ds(first + row, levels, stride=16), :]
            for g in range(3):
                out_ref[pl.ds(row * total + 3 * levels + g, 1), :] = edge_ref[
                    pl.ds(16 * g + first + row, 1), :
                ]
            out_ref[pl.ds(row * total + 3 * levels + 3, 1), :] = inv_ref[pl.ds(first + row, 1), :]
    pair = lax.broadcasted_iota(jnp.int32, (16, LANES), 1) >> 1
    low_base = 2 * total + 4

    def place(acc, value, slot, side):
        moved = pltpu.roll(value, (2 * slot + 2 * side) % LANES, 1)
        return jnp.where(pair == slot, moved, acc)

    for field, halves in enumerate(fields):
        for side in range(2):
            acc = jnp.zeros((16, LANES), jnp.float32)
            for l in range(levels):
                acc = place(acc, halves[side][16 * l : 16 * l + 16, :], l, side)
            if field == 0:
                cols = slice(side * LANES, (side + 1) * LANES)
                for g in range(4):
                    value = edge_ref[16 * g : 16 * g + 16, cols] if g < 3 else inv_ref[:, cols]
                    acc = place(acc, value, levels + g, side)
            cols = slice(field * LANES, (field + 1) * LANES)
            whole = left_ref if side == 0 else right_ref
            whole[:, cols] = acc
            slot = 3 * side + field
            rows = pl.ds(low_base + 8 * (slot // 2), 8)
            cols = slice((slot % 2) * LANES, (slot % 2 + 1) * LANES)
            top_ref[rows, cols] = acc[:8]
            bot_ref[rows, cols] = acc[8:]


def pack(theta, vapor, divergence, edge, inv):
    levels = theta.shape[0] // 16
    total = 3 * levels + 4
    rows = jax.ShapeDtypeStruct((2 * total + 28, 256), jnp.float32)
    cols = jax.ShapeDtypeStruct((16, 3 * LANES), jnp.float32)
    sides = [pl.BlockSpec((16 * levels, LANES), lambda s, c=c: (0, c)) for c in range(2)]
    whole = lambda a: pl.BlockSpec(a.shape, lambda s: (0,) * len(a.shape))
    outs = (rows, rows, cols, cols)
    return pl.pallas_call(
        pack_kernel,
        grid=(1,),
        in_specs=sides * 3 + [whole(edge), whole(inv)],
        out_specs=[whole(o) for o in outs],
        out_shape=outs,
        name="pack",
    )(theta, theta, vapor, vapor, divergence, divergence, edge, inv)


def onehot_kernel(high, span_ref, out_ref):
    def count(rows, shift):
        index = lax.broadcasted_iota(jnp.int32, (rows, 256), 0) - shift
        return index.astype(jnp.float32).astype(jnp.bfloat16)

    tall = count(high, high // 2)
    short = count(LANES, 0)
    one = jnp.bfloat16(1.0)
    zero = jnp.bfloat16(0.0)
    for r in range(span_ref.shape[0]):
        span = span_ref[r : r + 1, :]
        hi = ((span >> 7) - high // 2).astype(jnp.float32).astype(jnp.bfloat16)
        lo = (span & 127).astype(jnp.float32).astype(jnp.bfloat16)
        cols = slice(r * 256, (r + 1) * 256)
        out_ref[:high, cols] = jnp.where(tall == hi, one, zero)
        out_ref[high:, cols] = jnp.where(short == lo, one, zero)


def onehot(span, high):
    shape = jax.ShapeDtypeStruct((high + LANES, 4096), jnp.bfloat16)
    return pl.pallas_call(
        functools.partial(onehot_kernel, high),
        grid=(2,),
        in_specs=[pl.BlockSpec((8, 256), lambda s: (s, 0))],
        out_specs=pl.BlockSpec((high + LANES, 2048), lambda s: (0, s)),
        out_shape=shape,
        name="onehot",
        cost_estimate=pl.CostEstimate(flops=10**9, transcendentals=0, bytes_accessed=5 * 2**20),
    )(span)


def up(v):
    return pltpu.roll(v, v.shape[0] - 1, 0)


def down(v):
    return pltpu.roll(v, 1, 0)


def ahead(v):
    return pltpu.roll(v, v.shape[1] - 1, 1)


def behind(v):
    return pltpu.roll(v, 1, 1)


def main_kernel(
    peers, levels,
    damping_ref, exner_ref, scale_ref, mass_ref,
    theta_ref, vapor_ref, cloud_ref, div_ref, edge_ref, inv_ref, onehot_hbm,
    below_ref, above_ref, colr_ref, coll_ref, ownl_ref, ownr_ref,
    corner_below, corner_above,
    theta_out, vapor_out, cloud_out, div_out, send_out,
    coef_ref, edge_a, edge_b, rain_ref, onehot_ref, lo_ref, sem,
):
    total = 3 * levels + 4
    high = peers * 32
    step = pl.program_id(0)
    steps = pl.num_programs(0)
    fetch = pltpu.make_async_copy(onehot_hbm, onehot_ref, sem)

    sub = lax.broadcasted_iota(jnp.int32, (8, 256), 0)
    sub_half = sub[:, :LANES]

    def row_tile(index):
        def row(ref, r):
            return jnp.broadcast_to(ref[pl.ds(r * total + index, 1), :], (8, 256))

        low = jnp.where(sub < 1, row(below_ref, 0), row(below_ref, 1))
        top = jnp.where(sub < 7, row(above_ref, 0), row(above_ref, 1))
        tile = jnp.where(sub < 4, low, top)
        return tile[:, :LANES], tile[:, LANES:]

    @pl.when(step == 0)
    def _():
        fetch.start()
        lane24 = lax.broadcasted_iota(jnp.int32, (24, LANES), 1)
        even = (lane24 & 1) == 0

        def packed(own, low, top, cols):
            corner = jnp.where(sub_half < 4, low, top)
            return jnp.concatenate([own[:, cols], corner], axis=0)

        def side_packs(field):
            cols = slice(field * LANES, (field + 1) * LANES)

            def inner(ref, slot):
                rows = pl.ds(2 * total + 4 + 8 * (slot // 2), 8)
                return ref[rows, (slot % 2) * LANES : (slot % 2 + 1) * LANES]

            far = slice((3 + field) * LANES, (4 + field) * LANES)
            v_r = packed(colr_ref, corner_below[:, cols], corner_above[:, cols], cols)
            v_l = packed(coll_ref, corner_below[:, far], corner_above[:, far], cols)
            o_l = packed(ownl_ref, inner(below_ref, field), inner(above_ref, field), cols)
            o_r = packed(ownr_ref, inner(below_ref, 3 + field), inner(above_ref, 3 + field), cols)
            return v_r, v_l, o_l, o_r

        packs = [side_packs(field) for field in range(3)]
        geo = []
        for g in range(4):
            slot = levels + g
            right = pltpu.roll(packs[0][0], (LANES - 2 * slot) % LANES, 1)
            left = pltpu.roll(packs[0][1], (2 * LANES - 2 - 2 * slot) % LANES, 1)
            side = jnp.where(lane24 < 64, right, left)
            centre = edge_ref[16 * g : 16 * g + 16, :] if g < 3 else inv_ref[...]
            tiles = row_tile(3 * levels + g)
            halves = [
                jnp.concatenate([centre[:, h * LANES : (h + 1) * LANES], tiles[h]], axis=0)
                for h in range(2)
            ]
            geo.append(jnp.concatenate(halves + [side], axis=1))
        w0, w1, w2, inv = geo
        c1 = inv * w0
        c2 = inv * down(w0)
        c3 = inv * w1
        c4 = inv * behind(w1)
        c5 = inv * w2
        c6 = inv * behind(up(w2))
        c0 = c1 + c2 + c3 + c4 + c5 + c6
        shifted = (c0, c1, c2, behind(c3), ahead(c4), behind(c5), ahead(c6))
        for k, c in enumerate(shifted):
            coef_ref[k] = c[:, :256]
        rain_ref[...] = jnp.zeros_like(rain_ref)

        def pick(c, col):
            return jnp.broadcast_to(c[:, col : col + 1], (24, LANES))

        k0, k1, k2, k3, k4, k5, k6 = (
            jnp.where(even, pick(c, 256), pick(c, 383)) for c in (c0, c1, c2, c3, c4, c5, c6)
        )
        x3 = jnp.where(even, pick(c3, 255), pick(c4, 0))
        x5 = jnp.where(even, pick(c5, 255), 0.0)
        x6 = jnp.where(even, 0.0, pick(c6, 0))
        for field in range(3):
            v_r, v_l, o_l, o_r = packs[field]
            v = jnp.where(even, v_r, v_l)
            v_up = up(v)
            v_dn = down(v)
            edge_a[field] = x3 * v + x5 * v_dn + x6 * v_up
            nxt = jnp.where(even, ahead(v_r), behind(o_l))
            prv = jnp.where(even, ahead(o_r), behind(v_l))
            first = (k1 * v_up + k2 * v_dn - k0 * v) + (
                (k3 * nxt + k5 * down(nxt)) + (k4 * prv + k6 * up(prv))
            )
            edge_b[field] = x3 * first + x5 * down(first) + x6 * up(first)

    def lap(halves, edge, rows):
        lane = lax.broadcasted_iota(jnp.int32, (rows, LANES), 1)
        a, b, c = [], [], []
        for h in range(2):
            cols = slice(h * LANES, (h + 1) * LANES)
            v_up = up(halves[h])[:rows]
            v_dn = down(halves[h])[:rows]
            v = halves[h][:rows]
            a.append(ahead(coef_ref[3, :rows, cols] * v + coef_ref[5, :rows, cols] * v_dn))
            b.append(behind(coef_ref[4, :rows, cols] * v + coef_ref[6, :rows, cols] * v_up))
            c.append(
                coef_ref[1, :rows, cols] * v_up
                + coef_ref[2, :rows, cols] * v_dn
                - coef_ref[0, :rows, cols] * v
            )
        last = lane == LANES - 1
        zero = lane == 0
        left = (jnp.where(last, a[1], a[0]) + jnp.where(zero, edge, b[0])) + c[0]
        right = (jnp.where(last, edge, a[1]) + jnp.where(zero, b[0], b[1])) + c[1]
        return left, right

    def damp(ref, k, field, l):
        turn = lax.rem(2 * LANES - 1 - 2 * l, LANES)
        centre = [ref[k, :, h * LANES : (h + 1) * LANES] for h in range(2)]
        tiles = row_tile(field * levels + l)
        first = lap(
            [jnp.concatenate([centre[h], tiles[h]], axis=0) for h in range(2)],
            pltpu.roll(edge_a[field], turn, 1),
            24,
        )
        second = lap(first, pltpu.roll(edge_b[field, :16], turn, 1), 16)
        rate = damping_ref[field, l]
        return [centre[h] - rate * second[h] for h in range(2)]

    def level(k):
        l = step * BLOCK_LEVELS + k
        div = damp(div_ref, k, 2, l)
        thetas = damp(theta_ref, k, 0, l)
        vapors = damp(vapor_ref, k, 1, l)
        exner = exner_ref[l]
        scale = scale_ref[l]
        mass = mass_ref[l]
        ratio = jnp.full((1, LANES), LATENT, jnp.float32) / jnp.full((1, LANES), exner, jnp.float32)
        for h in range(2):
            cols = slice(h * LANES, (h + 1) * LANES)
            theta, vapor = thetas[h], vapors[h]
            div_out[k, :, cols] = div[h]
            cloud = cloud_ref[k, :, cols]
            temper = theta * exner
            saturation = scale * jnp.exp(temper)
            condensed = (vapor - saturation) / (1.0 + LATENT * saturation)
            saturation = scale * jnp.exp(temper + LATENT * condensed)
            condensed = condensed + (vapor - condensed - saturation) / (1.0 + LATENT * saturation)
            condensed = jnp.maximum(condensed, -cloud)
            theta_out[k, :, cols] = theta + condensed * ratio
            vapor_out[k, :, cols] = vapor - condensed
            liquid = cloud + condensed
            rained = AUTO_RATE * jnp.maximum(liquid - QCRIT, 0.0)
            cloud_out[k, :, cols] = liquid - rained
            rain_ref[:, cols] += mass * rained

    def body(m, carry):
        for j in range(UNROLL):
            level(m * UNROLL + j)
        return carry

    count = jnp.minimum(BLOCK_LEVELS, levels - step * BLOCK_LEVELS)
    lax.fori_loop(0, lax.div(count, UNROLL), body, 0)

    @pl.when(step == steps - 1)
    def _():
        fetch.wait()
        for r in range(16):
            value = rain_ref[r : r + 1, :]
            coarse = value.astype(jnp.bfloat16)
            fine = (value - coarse.astype(jnp.float32)).astype(jnp.bfloat16)
            cols = slice(r * 256, (r + 1) * 256)
            here = onehot_ref[high:, cols]
            lo_ref[:LANES, cols] = here * coarse
            lo_ref[LANES:, cols] = here * fine
        placed = lax.dot_general(
            onehot_ref[:high, :],
            lo_ref[...],
            (((1,), (1,)), ((), ())),
            preferred_element_type=jnp.float32,
        )
        send_out[...] = placed[:, :LANES] + placed[:, LANES:]


def physics(peers, scalars, fields, whole_args, marks, halos):
    levels = fields[0].shape[0]
    steps = pl.cdiv(levels, BLOCK_LEVELS)
    high = peers * 32
    block = pl.BlockSpec((BLOCK_LEVELS, 16, 256), lambda s: (s, 0, 0))
    whole = lambda a: pl.BlockSpec(a.shape, lambda s: (0,) * len(a.shape))
    field = jax.ShapeDtypeStruct(fields[0].shape, jnp.float32)
    sent = jax.ShapeDtypeStruct((high, LANES), jnp.float32)
    return pl.pallas_call(
        functools.partial(main_kernel, peers, levels),
        grid=(steps,),
        in_specs=[pl.BlockSpec(memory_space=pltpu.SMEM)] * 4
        + [block] * 4
        + [whole(a) for a in whole_args]
        + [pl.BlockSpec(memory_space=pl.ANY)]
        + [pl.BlockSpec(memory_space=pltpu.VMEM)] * 4
        + [whole(a) for a in halos[4:6]]
        + [pl.BlockSpec(memory_space=pltpu.VMEM)] * 2,
        out_specs=[block, block, block, block, whole(sent)],
        out_shape=[field, field, field, field, sent],
        scratch_shapes=[
            pltpu.VMEM((7, 24, 256), jnp.float32),
            pltpu.VMEM((3, 24, LANES), jnp.float32),
            pltpu.VMEM((3, 24, LANES), jnp.float32),
            pltpu.VMEM((16, 256), jnp.float32),
            pltpu.VMEM((high + LANES, 4096), jnp.bfloat16),
            pltpu.VMEM((2 * LANES, 4096), jnp.bfloat16),
            pltpu.SemaphoreType.DMA(()),
        ],
        name="physics",
    )(*scalars, *fields, *whole_args, marks, *halos)


def on_device(
    theta,
    vapor,
    cloud,
    divergence,
    edge_weight,
    inv_area,
    damping,
    exner,
    sat_scale,
    layer_mass,
    span_of,
):
    peers = lax.axis_size("py")

    def fetch(x, axis, step):
        count = lax.axis_size(axis)
        return lax.ppermute(x, axis, [((i + step) % count, i) for i in range(count)])

    flat = lambda x: x.reshape(-1, 256)
    edge = flat(edge_weight)
    top, bot, left, right = pack(flat(theta), flat(vapor), flat(divergence), edge, inv_area)
    colr = fetch(left, "py", 1)
    coll = fetch(right, "py", -1)
    below = fetch(top, "px", 1)
    above = fetch(bot, "px", -1)
    sides = jnp.concatenate([colr, coll], axis=1)
    corner_below = fetch(sides[:8], "px", 1)
    corner_above = fetch(sides[8:], "px", -1)
    halos = tuple(
        pltpu.with_memory_space_constraint(x, pltpu.VMEM)
        for x in (below, above, colr, coll, corner_below, corner_above)
    )
    marks = onehot(span_of, peers * 32)
    theta_next, vapor_next, cloud_next, divergence_next, send = physics(
        peers,
        (damping, exner, sat_scale, layer_mass),
        (theta, vapor, cloud, divergence),
        (edge, inv_area),
        marks,
        halos[:4] + (left, right) + halos[4:],
    )
    got = lax.all_to_all(send.reshape(peers, 32, LANES), "py", split_axis=0, concat_axis=0, tiled=True)
    precip = jnp.sum(got, axis=0).reshape(1, 4096)
    return (theta_next, vapor_next, cloud_next, divergence_next, precip)


def solution(mesh):
    field = P(None, "px", "py")
    plane = P("px", "py")
    return jax.shard_map(
        on_device,
        mesh=mesh,
        in_specs=(field, field, field, field, field, plane, P(), P(), P(), P(), plane),
        out_specs=(field, field, field, field, plane),
        check_vma=False,
    )
```

```python
import functools

import jax
import jax.numpy as jnp
from jax import lax
from jax.experimental import pallas as pl
from jax.experimental.pallas import tpu as pltpu
from jax.sharding import PartitionSpec as P

LATENT = 0.5
QCRIT = 0.2
AUTO_RATE = 0.5

LANES = 128
BLOCK_LEVELS = 16
UNROLL = 2


def pack_kernel(
    theta0, theta1, vapor0, vapor1, div0, div1, edge_ref, inv_ref,
    top_ref, bot_ref, left_ref, right_ref,
):
    levels = theta0.shape[0] // 16
    total = 3 * levels + 4
    fields = ((theta0, theta1), (vapor0, vapor1), (div0, div1))
    for out_ref, first in ((top_ref, 0), (bot_ref, 14)):
        for row in range(2):
            for field, halves in enumerate(fields):
                at = pl.ds(row * total + field * levels, levels)
                for half, ref in enumerate(halves):
                    cols = slice(half * LANES, (half + 1) * LANES)
                    out_ref[at, cols] = ref[pl.ds(first + row, levels, stride=16), :]
            for g in range(3):
                out_ref[pl.ds(row * total + 3 * levels + g, 1), :] = edge_ref[
                    pl.ds(16 * g + first + row, 1), :
                ]
            out_ref[pl.ds(row * total + 3 * levels + 3, 1), :] = inv_ref[pl.ds(first + row, 1), :]
    pair = lax.broadcasted_iota(jnp.int32, (16, LANES), 1) >> 1
    low_base = 2 * total + 4

    def place(acc, value, slot, side):
        moved = pltpu.roll(value, (2 * slot + 2 * side) % LANES, 1)
        return jnp.where(pair == slot, moved, acc)

    for field, halves in enumerate(fields):
        for side in range(2):
            acc = jnp.zeros((16, LANES), jnp.float32)
            for l in range(levels):
                acc = place(acc, halves[side][16 * l : 16 * l + 16, :], l, side)
            if field == 0:
                cols = slice(side * LANES, (side + 1) * LANES)
                for g in range(4):
                    value = edge_ref[16 * g : 16 * g + 16, cols] if g < 3 else inv_ref[:, cols]
                    acc = place(acc, value, levels + g, side)
            cols = slice(field * LANES, (field + 1) * LANES)
            whole = left_ref if side == 0 else right_ref
            whole[:, cols] = acc
            slot = 3 * side + field
            rows = pl.ds(low_base + 8 * (slot // 2), 8)
            cols = slice((slot % 2) * LANES, (slot % 2 + 1) * LANES)
            top_ref[rows, cols] = acc[:8]
            bot_ref[rows, cols] = acc[8:]


def pack(theta, vapor, divergence, edge, inv):
    levels = theta.shape[0] // 16
    total = 3 * levels + 4
    rows = jax.ShapeDtypeStruct((2 * total + 28, 256), jnp.float32)
    cols = jax.ShapeDtypeStruct((16, 3 * LANES), jnp.float32)
    sides = [pl.BlockSpec((16 * levels, LANES), lambda s, c=c: (0, c)) for c in range(2)]
    whole = lambda a: pl.BlockSpec(a.shape, lambda s: (0,) * len(a.shape))
    outs = (rows, rows, cols, cols)
    return pl.pallas_call(
        pack_kernel,
        grid=(1,),
        in_specs=sides * 3 + [whole(edge), whole(inv)],
        out_specs=[whole(o) for o in outs],
        out_shape=outs,
        name="pack",
        compiler_params=pltpu.CompilerParams(vmem_limit_bytes=32 * 2**20),
    )(theta, theta, vapor, vapor, divergence, divergence, edge, inv)


def onehot_kernel(high, span_ref, out_ref):
    def count(rows, shift):
        index = lax.broadcasted_iota(jnp.int32, (rows, 256), 0) - shift
        return index.astype(jnp.float32).astype(jnp.bfloat16)

    tall = count(high, high // 2)
    short = count(LANES, 0)
    one = jnp.bfloat16(1.0)
    zero = jnp.bfloat16(0.0)
    for r in range(span_ref.shape[0]):
        span = span_ref[r : r + 1, :]
        hi = ((span >> 7) - high // 2).astype(jnp.float32).astype(jnp.bfloat16)
        lo = (span & 127).astype(jnp.float32).astype(jnp.bfloat16)
        cols = slice(r * 256, (r + 1) * 256)
        out_ref[:high, cols] = jnp.where(tall == hi, one, zero)
        out_ref[high:, cols] = jnp.where(short == lo, one, zero)


def onehot(span, high):
    shape = jax.ShapeDtypeStruct((high + LANES, 4096), jnp.bfloat16)
    return pl.pallas_call(
        functools.partial(onehot_kernel, high),
        grid=(2,),
        in_specs=[pl.BlockSpec((8, 256), lambda s: (s, 0))],
        out_specs=pl.BlockSpec((high + LANES, 2048), lambda s: (0, s)),
        out_shape=shape,
        name="onehot",
        compiler_params=pltpu.CompilerParams(vmem_limit_bytes=32 * 2**20),
        cost_estimate=pl.CostEstimate(flops=10**9, transcendentals=0, bytes_accessed=5 * 2**20),
    )(span)


def up(v):
    return pltpu.roll(v, v.shape[0] - 1, 0)


def down(v):
    return pltpu.roll(v, 1, 0)


def ahead(v):
    return pltpu.roll(v, v.shape[1] - 1, 1)


def behind(v):
    return pltpu.roll(v, 1, 1)


def main_kernel(peers, levels, wet, *refs):
    total = 3 * levels + 4
    high = peers * 32
    step = pl.program_id(0)
    steps = pl.num_programs(0)
    if wet:
        damping_ref, exner_ref, scale_ref, mass_ref, theta_ref, vapor_ref, cloud_ref = refs[:7]
        onehot_ref = refs[7]
        theta_out, vapor_out, cloud_out, send_out = refs[18:22]
        coef_ref, edge_a, edge_b, rain_ref, lo_ref = refs[22:]
        halo_refs = refs[8:18]
    else:
        damping_ref, div_ref = refs[:2]
        halo_refs = refs[2:12]
        div_out, coef_ref, edge_a, edge_b = refs[12:]
    edge_ref, inv_ref, below_ref, above_ref, colr_ref, coll_ref = halo_refs[:6]
    ownl_ref, ownr_ref, corner_below, corner_above = halo_refs[6:]
    kinds = (0, 1) if wet else (2,)

    sub = lax.broadcasted_iota(jnp.int32, (8, 256), 0)
    sub_half = sub[:, :LANES]

    def row_tile(index):
        def row(ref, r):
            return jnp.broadcast_to(ref[pl.ds(r * total + index, 1), :], (8, 256))

        low = jnp.where(sub < 1, row(below_ref, 0), row(below_ref, 1))
        top = jnp.where(sub < 7, row(above_ref, 0), row(above_ref, 1))
        tile = jnp.where(sub < 4, low, top)
        return tile[:, :LANES], tile[:, LANES:]

    @pl.when(step == 0)
    def _():
        lane24 = lax.broadcasted_iota(jnp.int32, (24, LANES), 1)
        even = (lane24 & 1) == 0

        def packed(own, low, top, cols):
            corner = jnp.where(sub_half < 4, low, top)
            return jnp.concatenate([own[:, cols], corner], axis=0)

        def side_packs(field):
            cols = slice(field * LANES, (field + 1) * LANES)

            def inner(ref, slot):
                rows = pl.ds(2 * total + 4 + 8 * (slot // 2), 8)
                return ref[rows, (slot % 2) * LANES : (slot % 2 + 1) * LANES]

            far = slice((3 + field) * LANES, (4 + field) * LANES)
            v_r = packed(colr_ref, corner_below[:, cols], corner_above[:, cols], cols)
            v_l = packed(coll_ref, corner_below[:, far], corner_above[:, far], cols)
            o_l = packed(ownl_ref, inner(below_ref, field), inner(above_ref, field), cols)
            o_r = packed(ownr_ref, inner(below_ref, 3 + field), inner(above_ref, 3 + field), cols)
            return v_r, v_l, o_l, o_r

        packs = {field: side_packs(field) for field in {0, *kinds}}
        geo = []
        for g in range(4):
            slot = levels + g
            right = pltpu.roll(packs[0][0], (LANES - 2 * slot) % LANES, 1)
            left = pltpu.roll(packs[0][1], (2 * LANES - 2 - 2 * slot) % LANES, 1)
            side = jnp.where(lane24 < 64, right, left)
            centre = edge_ref[16 * g : 16 * g + 16, :] if g < 3 else inv_ref[...]
            tiles = row_tile(3 * levels + g)
            halves = [
                jnp.concatenate([centre[:, h * LANES : (h + 1) * LANES], tiles[h]], axis=0)
                for h in range(2)
            ]
            geo.append(jnp.concatenate(halves + [side], axis=1))
        w0, w1, w2, inv = geo
        c1 = inv * w0
        c2 = inv * down(w0)
        c3 = inv * w1
        c4 = inv * behind(w1)
        c5 = inv * w2
        c6 = inv * behind(up(w2))
        c0 = c1 + c2 + c3 + c4 + c5 + c6
        shifted = (c0, c1, c2, behind(c3), ahead(c4), behind(c5), ahead(c6))
        for k, c in enumerate(shifted):
            coef_ref[k] = c[:, :256]
        if wet:
            rain_ref[...] = jnp.zeros_like(rain_ref)

        def pick(c, col):
            return jnp.broadcast_to(c[:, col : col + 1], (24, LANES))

        k0, k1, k2, k3, k4, k5, k6 = (
            jnp.where(even, pick(c, 256), pick(c, 383)) for c in (c0, c1, c2, c3, c4, c5, c6)
        )
        x3 = jnp.where(even, pick(c3, 255), pick(c4, 0))
        x5 = jnp.where(even, pick(c5, 255), 0.0)
        x6 = jnp.where(even, 0.0, pick(c6, 0))
        for field in kinds:
            v_r, v_l, o_l, o_r = packs[field]
            v = jnp.where(even, v_r, v_l)
            v_up = up(v)
            v_dn = down(v)
            edge_a[field] = x3 * v + x5 * v_dn + x6 * v_up
            nxt = jnp.where(even, ahead(v_r), behind(o_l))
            prv = jnp.where(even, ahead(o_r), behind(v_l))
            first = (k1 * v_up + k2 * v_dn - k0 * v) + (
                (k3 * nxt + k5 * down(nxt)) + (k4 * prv + k6 * up(prv))
            )
            edge_b[field] = x3 * first + x5 * down(first) + x6 * up(first)

    def lap(halves, edge, rows):
        lane = lax.broadcasted_iota(jnp.int32, (rows, LANES), 1)
        a, b, c = [], [], []
        for h in range(2):
            cols = slice(h * LANES, (h + 1) * LANES)
            v_up = up(halves[h])[:rows]
            v_dn = down(halves[h])[:rows]
            v = halves[h][:rows]
            a.append(ahead(coef_ref[3, :rows, cols] * v + coef_ref[5, :rows, cols] * v_dn))
            b.append(behind(coef_ref[4, :rows, cols] * v + coef_ref[6, :rows, cols] * v_up))
            c.append(
                coef_ref[1, :rows, cols] * v_up
                + coef_ref[2, :rows, cols] * v_dn
                - coef_ref[0, :rows, cols] * v
            )
        last = lane == LANES - 1
        zero = lane == 0
        left = (jnp.where(last, a[1], a[0]) + jnp.where(zero, edge, b[0])) + c[0]
        right = (jnp.where(last, edge, a[1]) + jnp.where(zero, b[0], b[1])) + c[1]
        return left, right

    def damp(ref, k, field, l):
        turn = lax.rem(2 * LANES - 1 - 2 * l, LANES)
        centre = [ref[k, :, h * LANES : (h + 1) * LANES] for h in range(2)]
        tiles = row_tile(field * levels + l)
        first = lap(
            [jnp.concatenate([centre[h], tiles[h]], axis=0) for h in range(2)],
            pltpu.roll(edge_a[field], turn, 1),
            24,
        )
        second = lap(first, pltpu.roll(edge_b[field, :16], turn, 1), 16)
        rate = damping_ref[field, l]
        return [centre[h] - rate * second[h] for h in range(2)]

    def dry(k):
        div = damp(div_ref, k, 2, step * BLOCK_LEVELS + k)
        for h in range(2):
            div_out[k, :, h * LANES : (h + 1) * LANES] = div[h]

    def moist(k):
        l = step * BLOCK_LEVELS + k
        thetas = damp(theta_ref, k, 0, l)
        vapors = damp(vapor_ref, k, 1, l)
        exner = exner_ref[l]
        scale = scale_ref[l]
        mass = mass_ref[l]
        ratio = jnp.full((1, LANES), LATENT, jnp.float32) / jnp.full((1, LANES), exner, jnp.float32)
        for h in range(2):
            cols = slice(h * LANES, (h + 1) * LANES)
            theta, vapor = thetas[h], vapors[h]
            cloud = cloud_ref[k, :, cols]
            temper = theta * exner
            saturation = scale * jnp.exp(temper)
            condensed = (vapor - saturation) / (1.0 + LATENT * saturation)
            saturation = scale * jnp.exp(temper + LATENT * condensed)
            condensed = condensed + (vapor - condensed - saturation) / (1.0 + LATENT * saturation)
            condensed = jnp.maximum(condensed, -cloud)
            theta_out[k, :, cols] = theta + condensed * ratio
            vapor_out[k, :, cols] = vapor - condensed
            liquid = cloud + condensed
            rained = AUTO_RATE * jnp.maximum(liquid - QCRIT, 0.0)
            cloud_out[k, :, cols] = liquid - rained
            rain_ref[:, cols] += mass * rained

    def body(m, carry):
        for j in range(UNROLL):
            (moist if wet else dry)(m * UNROLL + j)
        return carry

    count = jnp.minimum(BLOCK_LEVELS, levels - step * BLOCK_LEVELS)
    lax.fori_loop(0, lax.div(count, UNROLL), body, 0)

    if not wet:
        return

    @pl.when(step == steps - 1)
    def _():
        for r in range(16):
            value = rain_ref[r : r + 1, :]
            coarse = value.astype(jnp.bfloat16)
            fine = (value - coarse.astype(jnp.float32)).astype(jnp.bfloat16)
            cols = slice(r * 256, (r + 1) * 256)
            here = onehot_ref[high:, cols]
            lo_ref[:LANES, cols] = here * coarse
            lo_ref[LANES:, cols] = here * fine
        placed = lax.dot_general(
            onehot_ref[:high, :],
            lo_ref[...],
            (((1,), (1,)), ((), ())),
            preferred_element_type=jnp.float32,
        )
        send_out[...] = placed[:, :LANES] + placed[:, LANES:]


SMEM = pl.BlockSpec(memory_space=pltpu.SMEM)
VMEM = pl.BlockSpec(memory_space=pltpu.VMEM)


def whole(a):
    return pl.BlockSpec(a.shape, lambda s: (0,) * len(a.shape))


def update(peers, wet, scalars, fields, marks, geometry, halos):
    levels = fields[0].shape[0]
    high = peers * 32
    block = pl.BlockSpec((BLOCK_LEVELS, 16, 256), lambda s: (s, 0, 0))
    field = jax.ShapeDtypeStruct(fields[0].shape, jnp.float32)
    sent = jax.ShapeDtypeStruct((high, LANES), jnp.float32)
    scratch = [
        pltpu.VMEM((7, 24, 256), jnp.float32),
        pltpu.VMEM((3, 24, LANES), jnp.float32),
        pltpu.VMEM((3, 24, LANES), jnp.float32),
    ]
    out_shape = [field] * len(fields)
    out_specs = [block] * len(fields)
    if wet:
        out_shape.append(sent)
        out_specs.append(whole(sent))
        scratch.append(pltpu.VMEM((16, 256), jnp.float32))
        scratch.append(pltpu.VMEM((2 * LANES, 4096), jnp.bfloat16))
    return pl.pallas_call(
        functools.partial(main_kernel, peers, levels, wet),
        grid=(pl.cdiv(levels, BLOCK_LEVELS),),
        in_specs=[SMEM] * len(scalars)
        + [block] * len(fields)
        + [VMEM] * len(marks)
        + [whole(a) for a in geometry]
        + [VMEM] * 4
        + [whole(a) for a in halos[4:6]]
        + [VMEM] * 2,
        out_specs=out_specs,
        out_shape=out_shape,
        scratch_shapes=scratch,
        name="moist" if wet else "dry",
        compiler_params=pltpu.CompilerParams(vmem_limit_bytes=32 * 2**20),
        cost_estimate=pl.CostEstimate(
            flops=10**8 * len(fields), transcendentals=0, bytes_accessed=2 * 2**20 * len(fields)
        ),
    )(*scalars, *fields, *marks, *geometry, *halos)


def on_device(
    theta,
    vapor,
    cloud,
    divergence,
    edge_weight,
    inv_area,
    damping,
    exner,
    sat_scale,
    layer_mass,
    span_of,
):
    peers = lax.axis_size("py")

    def fetch(x, axis, step):
        count = lax.axis_size(axis)
        return lax.ppermute(x, axis, [((i + step) % count, i) for i in range(count)])

    flat = lambda x: x.reshape(-1, 256)
    edge = flat(edge_weight)
    top, bot, left, right = pack(flat(theta), flat(vapor), flat(divergence), edge, inv_area)
    colr = fetch(left, "py", 1)
    coll = fetch(right, "py", -1)
    below = fetch(top, "px", 1)
    above = fetch(bot, "px", -1)
    marks = pltpu.with_memory_space_constraint(onehot(span_of, peers * 32), pltpu.VMEM)
    colr, coll, marks = lax.optimization_barrier((colr, coll, marks))
    sides = jnp.concatenate([colr, coll], axis=1)
    corner_below = fetch(sides[:8], "px", 1)
    corner_above = fetch(sides[8:], "px", -1)
    halos = tuple(
        pltpu.with_memory_space_constraint(x, pltpu.VMEM)
        for x in (below, above, colr, coll, corner_below, corner_above)
    )
    halos = halos[:4] + (left, right) + halos[4:]
    geometry = (edge, inv_area)
    theta_next, vapor_next, cloud_next, send = update(
        peers,
        True,
        (damping, exner, sat_scale, layer_mass),
        (theta, vapor, cloud),
        (marks,),
        geometry,
        halos,
    )
    got = lax.all_to_all(send.reshape(peers, 32, LANES), "py", split_axis=0, concat_axis=0, tiled=True)
    (divergence_next,) = update(
        peers, False, (damping,), (divergence,), (), geometry, halos
    )
    precip = jnp.sum(got, axis=0).reshape(1, 4096)
    return (theta_next, vapor_next, cloud_next, divergence_next, precip)


def solution(mesh):
    field = P(None, "px", "py")
    plane = P("px", "py")
    return jax.shard_map(
        on_device,
        mesh=mesh,
        in_specs=(field, field, field, field, field, plane, P(), P(), P(), P(), plane),
        out_specs=(field, field, field, field, plane),
        check_vma=False,
    )
```

```python
import functools

import jax
import jax.numpy as jnp
from jax import lax
from jax.experimental import pallas as pl
from jax.experimental.pallas import tpu as pltpu
from jax.sharding import PartitionSpec as P

LATENT = 0.5
QCRIT = 0.2
AUTO_RATE = 0.5

LANES = 128
BLOCK_LEVELS = 16
WET_UNROLL = 4
DRY_UNROLL = 2


def pack_kernel(
    theta_hbm, vapor_hbm, div_hbm, edge_hbm, inv_hbm,
    top_ref, bot_ref, left_ref, right_ref,
    theta0, theta1, vapor0, vapor1, div0, div1, edge_ref, inv_ref, sems,
):
    levels = theta0.shape[0] // 16
    total = 3 * levels + 4
    fields = ((theta0, theta1), (vapor0, vapor1), (div0, div1))
    copies = []
    for field, source in enumerate((theta_hbm, vapor_hbm, div_hbm)):
        for half, ref in enumerate(fields[field]):
            part = source.at[:, half * LANES : (half + 1) * LANES]
            copies.append(pltpu.make_async_copy(part, ref, sems.at[2 * field + half]))
    geometry = [
        pltpu.make_async_copy(edge_hbm, edge_ref, sems.at[6]),
        pltpu.make_async_copy(inv_hbm, inv_ref, sems.at[7]),
    ]
    for copy in geometry + copies:
        copy.start()
    for copy in geometry:
        copy.wait()
    for out_ref, first in ((top_ref, 0), (bot_ref, 14)):
        for row in range(2):
            for g in range(3):
                out_ref[pl.ds(row * total + 3 * levels + g, 1), :] = edge_ref[
                    pl.ds(16 * g + first + row, 1), :
                ]
            out_ref[pl.ds(row * total + 3 * levels + 3, 1), :] = inv_ref[pl.ds(first + row, 1), :]
    pair = lax.broadcasted_iota(jnp.int32, (16, LANES), 1) >> 1
    low_base = 2 * total + 4

    def place(acc, value, slot, side):
        moved = pltpu.roll(value, (2 * slot + 2 * side) % LANES, 1)
        return jnp.where(pair == slot, moved, acc)

    for field, halves in enumerate(fields):
        for side in range(2):
            copies[2 * field + side].wait()
            cols = slice(side * LANES, (side + 1) * LANES)
            for out_ref, first in ((top_ref, 0), (bot_ref, 14)):
                for row in range(2):
                    out_ref[pl.ds(row * total + field * levels, levels), cols] = halves[side][
                        pl.ds(first + row, levels, stride=16), :
                    ]
            acc = jnp.zeros((16, LANES), jnp.float32)
            for l in range(levels):
                acc = place(acc, halves[side][16 * l : 16 * l + 16, :], l, side)
            if field == 0:
                cols = slice(side * LANES, (side + 1) * LANES)
                for g in range(4):
                    value = edge_ref[16 * g : 16 * g + 16, cols] if g < 3 else inv_ref[:, cols]
                    acc = place(acc, value, levels + g, side)
            cols = slice(field * LANES, (field + 1) * LANES)
            whole = left_ref if side == 0 else right_ref
            whole[:, cols] = acc
            slot = 3 * side + field
            rows = pl.ds(low_base + 8 * (slot // 2), 8)
            cols = slice((slot % 2) * LANES, (slot % 2 + 1) * LANES)
            top_ref[rows, cols] = acc[:8]
            bot_ref[rows, cols] = acc[8:]


def pack(theta, vapor, divergence, edge, inv):
    levels = theta.shape[0] // 16
    total = 3 * levels + 4
    rows = jax.ShapeDtypeStruct((2 * total + 28, 256), jnp.float32)
    cols = jax.ShapeDtypeStruct((16, 3 * LANES), jnp.float32)
    outs = (rows, rows, cols, cols)
    vmem = pl.BlockSpec(memory_space=pltpu.VMEM)
    return pl.pallas_call(
        pack_kernel,
        in_specs=[pl.BlockSpec(memory_space=pltpu.HBM)] * 5,
        out_specs=[vmem] * 4,
        out_shape=outs,
        scratch_shapes=[pltpu.VMEM((16 * levels, LANES), jnp.float32)] * 6
        + [
            pltpu.VMEM(edge.shape, jnp.float32),
            pltpu.VMEM(inv.shape, jnp.float32),
            pltpu.SemaphoreType.DMA((8,)),
        ],
        name="pack",
        compiler_params=pltpu.CompilerParams(vmem_limit_bytes=32 * 2**20),
    )(theta, vapor, divergence, edge, inv)


def onehot_kernel(high, span_ref, out_ref):
    def count(rows, shift):
        index = lax.broadcasted_iota(jnp.int32, (rows, 256), 0) - shift
        return index.astype(jnp.float32).astype(jnp.bfloat16)

    tall = count(high, high // 2)
    short = count(LANES, 0)
    one = jnp.bfloat16(1.0)
    zero = jnp.bfloat16(0.0)
    for r in range(span_ref.shape[0]):
        span = span_ref[r : r + 1, :]
        hi = ((span >> 7) - high // 2).astype(jnp.float32).astype(jnp.bfloat16)
        lo = (span & 127).astype(jnp.float32).astype(jnp.bfloat16)
        cols = slice(r * 256, (r + 1) * 256)
        out_ref[:high, cols] = jnp.where(tall == hi, one, zero)
        out_ref[high:, cols] = jnp.where(short == lo, one, zero)


def onehot(span, high):
    shape = jax.ShapeDtypeStruct((high + LANES, 4096), jnp.bfloat16)
    return pl.pallas_call(
        functools.partial(onehot_kernel, high),
        grid=(2,),
        in_specs=[pl.BlockSpec((8, 256), lambda s: (s, 0))],
        out_specs=pl.BlockSpec((high + LANES, 2048), lambda s: (0, s)),
        out_shape=shape,
        name="onehot",
        compiler_params=pltpu.CompilerParams(vmem_limit_bytes=32 * 2**20),
        cost_estimate=pl.CostEstimate(flops=10**9, transcendentals=0, bytes_accessed=5 * 2**20),
    )(span)


def up(v):
    return pltpu.roll(v, v.shape[0] - 1, 0)


def down(v):
    return pltpu.roll(v, 1, 0)


def ahead(v):
    return pltpu.roll(v, v.shape[1] - 1, 1)


def behind(v):
    return pltpu.roll(v, 1, 1)


def main_kernel(peers, levels, wet, *refs):
    total = 3 * levels + 4
    high = peers * 32
    step = pl.program_id(0)
    steps = pl.num_programs(0)
    if wet:
        damping_ref, exner_ref, scale_ref, mass_ref, theta_ref, vapor_ref, cloud_ref = refs[:7]
        onehot_ref = refs[7]
        theta_out, vapor_out, cloud_out, send_out = refs[18:22]
        coef_ref, edge_a, edge_b, rain_ref, lo_ref = refs[22:]
        halo_refs = refs[8:18]
    else:
        damping_ref, div_ref = refs[:2]
        halo_refs = refs[2:12]
        div_out, coef_ref, edge_a, edge_b = refs[12:]
    edge_ref, inv_ref, below_ref, above_ref, colr_ref, coll_ref = halo_refs[:6]
    ownl_ref, ownr_ref, corner_below, corner_above = halo_refs[6:]
    kinds = (0, 1) if wet else (2,)

    sub = lax.broadcasted_iota(jnp.int32, (8, 256), 0)
    sub_half = sub[:, :LANES]

    def row_tile(index):
        def row(ref, r):
            return jnp.broadcast_to(ref[pl.ds(r * total + index, 1), :], (8, 256))

        low = jnp.where(sub < 1, row(below_ref, 0), row(below_ref, 1))
        top = jnp.where(sub < 7, row(above_ref, 0), row(above_ref, 1))
        tile = jnp.where(sub < 4, low, top)
        return tile[:, :LANES], tile[:, LANES:]

    @pl.when(step == 0)
    def _():
        lane24 = lax.broadcasted_iota(jnp.int32, (24, LANES), 1)
        even = (lane24 & 1) == 0

        def packed(own, low, top, cols):
            corner = jnp.where(sub_half < 4, low, top)
            return jnp.concatenate([own[:, cols], corner], axis=0)

        def side_packs(field):
            cols = slice(field * LANES, (field + 1) * LANES)

            def inner(ref, slot):
                rows = pl.ds(2 * total + 4 + 8 * (slot // 2), 8)
                return ref[rows, (slot % 2) * LANES : (slot % 2 + 1) * LANES]

            far = slice((3 + field) * LANES, (4 + field) * LANES)
            v_r = packed(colr_ref, corner_below[:, cols], corner_above[:, cols], cols)
            v_l = packed(coll_ref, corner_below[:, far], corner_above[:, far], cols)
            o_l = packed(ownl_ref, inner(below_ref, field), inner(above_ref, field), cols)
            o_r = packed(ownr_ref, inner(below_ref, 3 + field), inner(above_ref, 3 + field), cols)
            return v_r, v_l, o_l, o_r

        packs = {field: side_packs(field) for field in {0, *kinds}}
        geo = []
        for g in range(4):
            slot = levels + g
            right = pltpu.roll(packs[0][0], (LANES - 2 * slot) % LANES, 1)
            left = pltpu.roll(packs[0][1], (2 * LANES - 2 - 2 * slot) % LANES, 1)
            side = jnp.where(lane24 < 64, right, left)
            centre = edge_ref[16 * g : 16 * g + 16, :] if g < 3 else inv_ref[...]
            tiles = row_tile(3 * levels + g)
            halves = [
                jnp.concatenate([centre[:, h * LANES : (h + 1) * LANES], tiles[h]], axis=0)
                for h in range(2)
            ]
            geo.append(jnp.concatenate(halves + [side], axis=1))
        w0, w1, w2, inv = geo
        c1 = inv * w0
        c2 = inv * down(w0)
        c3 = inv * w1
        c4 = inv * behind(w1)
        c5 = inv * w2
        c6 = inv * behind(up(w2))
        c0 = c1 + c2 + c3 + c4 + c5 + c6
        shifted = (c0, c1, c2, behind(c3), ahead(c4), behind(c5), ahead(c6))
        for k, c in enumerate(shifted):
            coef_ref[k] = c[:, :256]
        if wet:
            rain_ref[...] = jnp.zeros_like(rain_ref)

        def pick(c, col):
            return jnp.broadcast_to(c[:, col : col + 1], (24, LANES))

        k0, k1, k2, k3, k4, k5, k6 = (
            jnp.where(even, pick(c, 256), pick(c, 383)) for c in (c0, c1, c2, c3, c4, c5, c6)
        )
        x3 = jnp.where(even, pick(c3, 255), pick(c4, 0))
        x5 = jnp.where(even, pick(c5, 255), 0.0)
        x6 = jnp.where(even, 0.0, pick(c6, 0))
        for field in kinds:
            v_r, v_l, o_l, o_r = packs[field]
            v = jnp.where(even, v_r, v_l)
            v_up = up(v)
            v_dn = down(v)
            edge_a[field] = x3 * v + x5 * v_dn + x6 * v_up
            nxt = jnp.where(even, ahead(v_r), behind(o_l))
            prv = jnp.where(even, ahead(o_r), behind(v_l))
            first = (k1 * v_up + k2 * v_dn - k0 * v) + (
                (k3 * nxt + k5 * down(nxt)) + (k4 * prv + k6 * up(prv))
            )
            edge_b[field] = x3 * first + x5 * down(first) + x6 * up(first)

    def lap(halves, edge, rows):
        lane = lax.broadcasted_iota(jnp.int32, (rows, LANES), 1)
        a, b, c = [], [], []
        for h in range(2):
            cols = slice(h * LANES, (h + 1) * LANES)
            v_up = up(halves[h])[:rows]
            v_dn = down(halves[h])[:rows]
            v = halves[h][:rows]
            a.append(ahead(coef_ref[3, :rows, cols] * v + coef_ref[5, :rows, cols] * v_dn))
            b.append(behind(coef_ref[4, :rows, cols] * v + coef_ref[6, :rows, cols] * v_up))
            c.append(
                coef_ref[1, :rows, cols] * v_up
                + coef_ref[2, :rows, cols] * v_dn
                - coef_ref[0, :rows, cols] * v
            )
        last = lane == LANES - 1
        zero = lane == 0
        left = (jnp.where(last, a[1], a[0]) + jnp.where(zero, edge, b[0])) + c[0]
        right = (jnp.where(last, edge, a[1]) + jnp.where(zero, b[0], b[1])) + c[1]
        return left, right

    def damp(ref, k, field, l):
        turn = lax.rem(2 * LANES - 1 - 2 * l, LANES)
        centre = [ref[k, :, h * LANES : (h + 1) * LANES] for h in range(2)]
        tiles = row_tile(field * levels + l)
        first = lap(
            [jnp.concatenate([centre[h], tiles[h]], axis=0) for h in range(2)],
            pltpu.roll(edge_a[field], turn, 1),
            24,
        )
        second = lap(first, pltpu.roll(edge_b[field, :16], turn, 1), 16)
        rate = damping_ref[field, l]
        return [centre[h] - rate * second[h] for h in range(2)]

    def dry(k):
        div = damp(div_ref, k, 2, step * BLOCK_LEVELS + k)
        for h in range(2):
            div_out[k, :, h * LANES : (h + 1) * LANES] = div[h]

    def moist(k):
        l = step * BLOCK_LEVELS + k
        thetas = damp(theta_ref, k, 0, l)
        vapors = damp(vapor_ref, k, 1, l)
        exner = exner_ref[l]
        scale = scale_ref[l]
        mass = mass_ref[l]
        ratio = jnp.full((1, LANES), LATENT, jnp.float32) / jnp.full((1, LANES), exner, jnp.float32)
        for h in range(2):
            cols = slice(h * LANES, (h + 1) * LANES)
            theta, vapor = thetas[h], vapors[h]
            cloud = cloud_ref[k, :, cols]
            temper = theta * exner
            saturation = scale * jnp.exp(temper)
            condensed = (vapor - saturation) / (1.0 + LATENT * saturation)
            saturation = scale * jnp.exp(temper + LATENT * condensed)
            condensed = condensed + (vapor - condensed - saturation) / (1.0 + LATENT * saturation)
            condensed = jnp.maximum(condensed, -cloud)
            theta_out[k, :, cols] = theta + condensed * ratio
            vapor_out[k, :, cols] = vapor - condensed
            liquid = cloud + condensed
            rained = AUTO_RATE * jnp.maximum(liquid - QCRIT, 0.0)
            cloud_out[k, :, cols] = liquid - rained
            rain_ref[:, cols] += mass * rained

    count = jnp.minimum(BLOCK_LEVELS, levels - step * BLOCK_LEVELS)
    unroll = WET_UNROLL if wet else DRY_UNROLL

    def sweep(start, stop, width):
        def body(m, carry):
            for j in range(width):
                (moist if wet else dry)(m * width + j)
            return carry

        lax.fori_loop(start, stop, body, 0)

    full = lax.div(count, unroll)
    sweep(0, full, unroll)
    if unroll > 2:
        sweep(full * (unroll // 2), lax.div(count, 2), 2)

    if not wet:
        return

    @pl.when(step == steps - 1)
    def _():
        for r in range(16):
            value = rain_ref[r : r + 1, :]
            coarse = value.astype(jnp.bfloat16)
            fine = (value - coarse.astype(jnp.float32)).astype(jnp.bfloat16)
            cols = slice(r * 256, (r + 1) * 256)
            here = onehot_ref[high:, cols]
            lo_ref[:LANES, cols] = here * coarse
            lo_ref[LANES:, cols] = here * fine
        placed = lax.dot_general(
            onehot_ref[:high, :],
            lo_ref[...],
            (((1,), (1,)), ((), ())),
            preferred_element_type=jnp.float32,
        )
        send_out[...] = placed[:, :LANES] + placed[:, LANES:]


SMEM = pl.BlockSpec(memory_space=pltpu.SMEM)
VMEM = pl.BlockSpec(memory_space=pltpu.VMEM)


def whole(a):
    return pl.BlockSpec(a.shape, lambda s: (0,) * len(a.shape))


def update(peers, wet, scalars, fields, marks, geometry, halos):
    levels = fields[0].shape[0]
    high = peers * 32
    block = pl.BlockSpec((BLOCK_LEVELS, 16, 256), lambda s: (s, 0, 0))
    field = jax.ShapeDtypeStruct(fields[0].shape, jnp.float32)
    sent = jax.ShapeDtypeStruct((high, LANES), jnp.float32)
    scratch = [
        pltpu.VMEM((7, 24, 256), jnp.float32),
        pltpu.VMEM((3, 24, LANES), jnp.float32),
        pltpu.VMEM((3, 24, LANES), jnp.float32),
    ]
    out_shape = [field] * len(fields)
    out_specs = [block] * len(fields)
    if wet:
        out_shape.append(sent)
        out_specs.append(whole(sent))
        scratch.append(pltpu.VMEM((16, 256), jnp.float32))
        scratch.append(pltpu.VMEM((2 * LANES, 4096), jnp.bfloat16))
    return pl.pallas_call(
        functools.partial(main_kernel, peers, levels, wet),
        grid=(pl.cdiv(levels, BLOCK_LEVELS),),
        in_specs=[SMEM] * len(scalars)
        + [block] * len(fields)
        + [VMEM] * len(marks)
        + [whole(a) for a in geometry]
        + [VMEM] * 4
        + [whole(a) for a in halos[4:6]]
        + [VMEM] * 2,
        out_specs=out_specs,
        out_shape=out_shape,
        scratch_shapes=scratch,
        name="moist" if wet else "dry",
        compiler_params=pltpu.CompilerParams(vmem_limit_bytes=32 * 2**20),
        cost_estimate=pl.CostEstimate(
            flops=10**8 * len(fields), transcendentals=0, bytes_accessed=2 * 2**20 * len(fields)
        ),
    )(*scalars, *fields, *marks, *geometry, *halos)


def on_device(
    theta,
    vapor,
    cloud,
    divergence,
    edge_weight,
    inv_area,
    damping,
    exner,
    sat_scale,
    layer_mass,
    span_of,
):
    peers = lax.axis_size("py")

    def fetch(x, axis, step):
        count = lax.axis_size(axis)
        return lax.ppermute(x, axis, [((i + step) % count, i) for i in range(count)])

    flat = lambda x: x.reshape(-1, 256)
    edge = flat(edge_weight)
    top, bot, left, right = pack(
        *(
            pltpu.with_memory_space_constraint(flat(x), pltpu.HBM)
            for x in (theta, vapor, divergence, edge_weight, inv_area)
        )
    )
    colr = fetch(left, "py", 1)
    coll = fetch(right, "py", -1)
    below = fetch(top, "px", 1)
    above = fetch(bot, "px", -1)
    marks = pltpu.with_memory_space_constraint(onehot(span_of, peers * 32), pltpu.VMEM)
    colr, coll, marks = lax.optimization_barrier((colr, coll, marks))
    sides = jnp.concatenate([colr, coll], axis=1)
    corner_below = fetch(sides[:8], "px", 1)
    corner_above = fetch(sides[8:], "px", -1)
    halos = tuple(
        pltpu.with_memory_space_constraint(x, pltpu.VMEM)
        for x in (below, above, colr, coll, corner_below, corner_above)
    )
    halos = halos[:4] + (left, right) + halos[4:]
    geometry = (edge, inv_area)
    theta_next, vapor_next, cloud_next, send = update(
        peers,
        True,
        (damping, exner, sat_scale, layer_mass),
        (theta, vapor, cloud),
        (marks,),
        geometry,
        halos,
    )
    got = lax.all_to_all(send.reshape(peers, 32, LANES), "py", split_axis=0, concat_axis=0, tiled=True)
    (divergence_next,) = update(
        peers, False, (damping,), (divergence,), (), geometry, halos
    )
    precip = jnp.sum(got, axis=0).reshape(1, 4096)
    return (theta_next, vapor_next, cloud_next, divergence_next, precip)


def solution(mesh):
    field = P(None, "px", "py")
    plane = P("px", "py")
    return jax.shard_map(
        on_device,
        mesh=mesh,
        in_specs=(field, field, field, field, field, plane, P(), P(), P(), P(), plane),
        out_specs=(field, field, field, field, plane),
        check_vma=False,
    )
```

```python
import functools

import jax
import jax.numpy as jnp
from jax import lax
from jax.experimental import pallas as pl
from jax.experimental.pallas import tpu as pltpu
from jax.sharding import PartitionSpec as P

LATENT = 0.5
QCRIT = 0.2
AUTO_RATE = 0.5

LANES = 128
BLOCK_LEVELS = 16
WET_UNROLL = 4
DRY_UNROLL = 2


def pack_kernel(
    theta_hbm, vapor_hbm, div_hbm, edge_hbm, inv_hbm,
    top_ref, bot_ref, left_ref, right_ref,
    theta0, theta1, vapor0, vapor1, div0, div1, edge_ref, inv_ref, sems,
):
    levels = theta0.shape[0] // 16
    total = 3 * levels + 4
    fields = ((theta0, theta1), (vapor0, vapor1), (div0, div1))
    copies = []
    for field, source in enumerate((theta_hbm, vapor_hbm, div_hbm)):
        for half, ref in enumerate(fields[field]):
            part = source.at[:, half * LANES : (half + 1) * LANES]
            copies.append(pltpu.make_async_copy(part, ref, sems.at[2 * field + half]))
    geometry = [
        pltpu.make_async_copy(edge_hbm, edge_ref, sems.at[6]),
        pltpu.make_async_copy(inv_hbm, inv_ref, sems.at[7]),
    ]
    for copy in geometry + copies:
        copy.start()
    for copy in geometry:
        copy.wait()
    for out_ref, first in ((top_ref, 0), (bot_ref, 14)):
        for row in range(2):
            for g in range(3):
                out_ref[pl.ds(row * total + 3 * levels + g, 1), :] = edge_ref[
                    pl.ds(16 * g + first + row, 1), :
                ]
            out_ref[pl.ds(row * total + 3 * levels + 3, 1), :] = inv_ref[pl.ds(first + row, 1), :]
    pair = lax.broadcasted_iota(jnp.int32, (16, LANES), 1) >> 1
    low_base = 2 * total + 4

    def place(acc, value, slot, side):
        moved = pltpu.roll(value, (2 * slot + 2 * side) % LANES, 1)
        return jnp.where(pair == slot, moved, acc)

    for field, halves in enumerate(fields):
        for side in range(2):
            copies[2 * field + side].wait()
            cols = slice(side * LANES, (side + 1) * LANES)
            for out_ref, first in ((top_ref, 0), (bot_ref, 14)):
                for row in range(2):
                    out_ref[pl.ds(row * total + field * levels, levels), cols] = halves[side][
                        pl.ds(first + row, levels, stride=16), :
                    ]
            acc = jnp.zeros((16, LANES), jnp.float32)
            for l in range(levels):
                acc = place(acc, halves[side][16 * l : 16 * l + 16, :], l, side)
            if field == 0:
                cols = slice(side * LANES, (side + 1) * LANES)
                for g in range(4):
                    value = edge_ref[16 * g : 16 * g + 16, cols] if g < 3 else inv_ref[:, cols]
                    acc = place(acc, value, levels + g, side)
            cols = slice(field * LANES, (field + 1) * LANES)
            whole = left_ref if side == 0 else right_ref
            whole[:, cols] = acc
            slot = 3 * side + field
            rows = pl.ds(low_base + 8 * (slot // 2), 8)
            cols = slice((slot % 2) * LANES, (slot % 2 + 1) * LANES)
            top_ref[rows, cols] = acc[:8]
            bot_ref[rows, cols] = acc[8:]


def pack(theta, vapor, divergence, edge, inv):
    levels = theta.shape[0] // 16
    total = 3 * levels + 4
    rows = jax.ShapeDtypeStruct((2 * total + 28, 256), jnp.float32)
    cols = jax.ShapeDtypeStruct((16, 3 * LANES), jnp.float32)
    outs = (rows, rows, cols, cols)
    vmem = pl.BlockSpec(memory_space=pltpu.VMEM)
    return pl.pallas_call(
        pack_kernel,
        in_specs=[pl.BlockSpec(memory_space=pltpu.HBM)] * 5,
        out_specs=[vmem] * 4,
        out_shape=outs,
        scratch_shapes=[pltpu.VMEM((16 * levels, LANES), jnp.float32)] * 6
        + [
            pltpu.VMEM(edge.shape, jnp.float32),
            pltpu.VMEM(inv.shape, jnp.float32),
            pltpu.SemaphoreType.DMA((8,)),
        ],
        name="pack",
        compiler_params=pltpu.CompilerParams(vmem_limit_bytes=32 * 2**20),
    )(theta, vapor, divergence, edge, inv)


def onehot_kernel(high, span_ref, out_ref):
    def count(rows, shift):
        index = lax.broadcasted_iota(jnp.int32, (rows, 256), 0) - shift
        return index.astype(jnp.float32).astype(jnp.bfloat16)

    tall = count(high, high // 2)
    short = count(LANES, 0)
    one = jnp.bfloat16(1.0)
    zero = jnp.bfloat16(0.0)
    for r in range(span_ref.shape[0]):
        span = span_ref[r : r + 1, :]
        hi = ((span >> 7) - high // 2).astype(jnp.float32).astype(jnp.bfloat16)
        lo = (span & 127).astype(jnp.float32).astype(jnp.bfloat16)
        cols = slice(r * 256, (r + 1) * 256)
        out_ref[:high, cols] = jnp.where(tall == hi, one, zero)
        out_ref[high:, cols] = jnp.where(short == lo, one, zero)


def onehot(span, high):
    shape = jax.ShapeDtypeStruct((high + LANES, 4096), jnp.bfloat16)
    return pl.pallas_call(
        functools.partial(onehot_kernel, high),
        grid=(2,),
        in_specs=[pl.BlockSpec((8, 256), lambda s: (s, 0))],
        out_specs=pl.BlockSpec((high + LANES, 2048), lambda s: (0, s)),
        out_shape=shape,
        name="onehot",
        compiler_params=pltpu.CompilerParams(vmem_limit_bytes=32 * 2**20),
        cost_estimate=pl.CostEstimate(flops=10**9, transcendentals=0, bytes_accessed=5 * 2**20),
    )(span)


def up(v):
    return pltpu.roll(v, v.shape[0] - 1, 0)


def down(v):
    return pltpu.roll(v, 1, 0)


def ahead(v):
    return pltpu.roll(v, v.shape[1] - 1, 1)


def behind(v):
    return pltpu.roll(v, 1, 1)


def main_kernel(peers, levels, wet, *refs):
    total = 3 * levels + 4
    high = peers * 32
    step = pl.program_id(0)
    steps = pl.num_programs(0)
    if wet:
        damping_ref, exner_ref, scale_ref, mass_ref, theta_ref, vapor_ref, cloud_ref = refs[:7]
        onehot_ref = refs[7]
        theta_out, vapor_out, cloud_out, send_out = refs[18:22]
        coef_ref, edge_a, edge_b, rain_ref, lo_ref = refs[22:]
        halo_refs = refs[8:18]
    else:
        damping_ref, div_ref = refs[:2]
        halo_refs = refs[2:12]
        div_out, coef_ref, edge_a, edge_b = refs[12:]
    edge_ref, inv_ref, below_ref, above_ref, colr_ref, coll_ref = halo_refs[:6]
    ownl_ref, ownr_ref, corner_below, corner_above = halo_refs[6:]
    kinds = (0, 1) if wet else (2,)

    sub = lax.broadcasted_iota(jnp.int32, (8, 256), 0)
    sub_half = sub[:, :LANES]

    def row_tile(index):
        def row(ref, r):
            return jnp.broadcast_to(ref[pl.ds(r * total + index, 1), :], (8, 256))

        low = jnp.where(sub < 1, row(below_ref, 0), row(below_ref, 1))
        top = jnp.where(sub < 7, row(above_ref, 0), row(above_ref, 1))
        tile = jnp.where(sub < 4, low, top)
        return tile[:, :LANES], tile[:, LANES:]

    @pl.when(step == 0)
    def _():
        lane24 = lax.broadcasted_iota(jnp.int32, (24, LANES), 1)
        even = (lane24 & 1) == 0

        def packed(own, low, top, cols):
            corner = jnp.where(sub_half < 4, low, top)
            return jnp.concatenate([own[:, cols], corner], axis=0)

        def side_packs(field):
            cols = slice(field * LANES, (field + 1) * LANES)

            def inner(ref, slot):
                rows = pl.ds(2 * total + 4 + 8 * (slot // 2), 8)
                return ref[rows, (slot % 2) * LANES : (slot % 2 + 1) * LANES]

            far = slice((3 + field) * LANES, (4 + field) * LANES)
            v_r = packed(colr_ref, corner_below[:, cols], corner_above[:, cols], cols)
            v_l = packed(coll_ref, corner_below[:, far], corner_above[:, far], cols)
            o_l = packed(ownl_ref, inner(below_ref, field), inner(above_ref, field), cols)
            o_r = packed(ownr_ref, inner(below_ref, 3 + field), inner(above_ref, 3 + field), cols)
            return v_r, v_l, o_l, o_r

        packs = {field: side_packs(field) for field in {0, *kinds}}
        geo = []
        for g in range(4):
            slot = levels + g
            right = pltpu.roll(packs[0][0], (LANES - 2 * slot) % LANES, 1)
            left = pltpu.roll(packs[0][1], (2 * LANES - 2 - 2 * slot) % LANES, 1)
            side = jnp.where(lane24 < 64, right, left)
            centre = edge_ref[16 * g : 16 * g + 16, :] if g < 3 else inv_ref[...]
            tiles = row_tile(3 * levels + g)
            halves = [
                jnp.concatenate([centre[:, h * LANES : (h + 1) * LANES], tiles[h]], axis=0)
                for h in range(2)
            ]
            geo.append(jnp.concatenate(halves + [side], axis=1))
        w0, w1, w2, inv = geo
        c1 = inv * w0
        c2 = inv * down(w0)
        c3 = inv * w1
        c4 = inv * behind(w1)
        c5 = inv * w2
        c6 = inv * behind(up(w2))
        c0 = c1 + c2 + c3 + c4 + c5 + c6
        shifted = (c0, c1, c2, behind(c3), ahead(c4), behind(c5), ahead(c6))
        for k, c in enumerate(shifted):
            coef_ref[k] = c[:, :256]
        if wet:
            rain_ref[...] = jnp.zeros_like(rain_ref)

        def pick(c, col):
            return jnp.broadcast_to(c[:, col : col + 1], (24, LANES))

        k0, k1, k2, k3, k4, k5, k6 = (
            jnp.where(even, pick(c, 256), pick(c, 383)) for c in (c0, c1, c2, c3, c4, c5, c6)
        )
        x3 = jnp.where(even, pick(c3, 255), pick(c4, 0))
        x5 = jnp.where(even, pick(c5, 255), 0.0)
        x6 = jnp.where(even, 0.0, pick(c6, 0))
        for field in kinds:
            v_r, v_l, o_l, o_r = packs[field]
            v = jnp.where(even, v_r, v_l)
            v_up = up(v)
            v_dn = down(v)
            edge_a[field] = x3 * v + x5 * v_dn + x6 * v_up
            nxt = jnp.where(even, ahead(v_r), behind(o_l))
            prv = jnp.where(even, ahead(o_r), behind(v_l))
            first = (k1 * v_up + k2 * v_dn - k0 * v) + (
                (k3 * nxt + k5 * down(nxt)) + (k4 * prv + k6 * up(prv))
            )
            edge_b[field] = x3 * first + x5 * down(first) + x6 * up(first)

    def lap(halves, edge, rows):
        lane = lax.broadcasted_iota(jnp.int32, (rows, LANES), 1)
        a, b, c = [], [], []
        for h in range(2):
            cols = slice(h * LANES, (h + 1) * LANES)
            v_up = up(halves[h])[:rows]
            v_dn = down(halves[h])[:rows]
            v = halves[h][:rows]
            a.append(ahead(coef_ref[3, :rows, cols] * v + coef_ref[5, :rows, cols] * v_dn))
            b.append(behind(coef_ref[4, :rows, cols] * v + coef_ref[6, :rows, cols] * v_up))
            c.append(
                coef_ref[1, :rows, cols] * v_up
                + coef_ref[2, :rows, cols] * v_dn
                - coef_ref[0, :rows, cols] * v
            )
        last = lane == LANES - 1
        zero = lane == 0
        left = (jnp.where(last, a[1], a[0]) + jnp.where(zero, edge, b[0])) + c[0]
        right = (jnp.where(last, edge, a[1]) + jnp.where(zero, b[0], b[1])) + c[1]
        return left, right

    def damp(ref, field, l):
        turn = lax.rem(2 * LANES - 1 - 2 * l, LANES)
        centre = [ref[l, :, h * LANES : (h + 1) * LANES] for h in range(2)]
        tiles = row_tile(field * levels + l)
        first = lap(
            [jnp.concatenate([centre[h], tiles[h]], axis=0) for h in range(2)],
            pltpu.roll(edge_a[field], turn, 1),
            24,
        )
        second = lap(first, pltpu.roll(edge_b[field, :16], turn, 1), 16)
        rate = damping_ref[field, l]
        return [centre[h] - rate * second[h] for h in range(2)]

    def dry(k):
        div = damp(div_ref, 2, step * BLOCK_LEVELS + k)
        for h in range(2):
            div_out[k, :, h * LANES : (h + 1) * LANES] = div[h]

    def moist(k):
        l = step * BLOCK_LEVELS + k
        thetas = damp(theta_ref, 0, l)
        vapors = damp(vapor_ref, 1, l)
        exner = exner_ref[l]
        scale = scale_ref[l]
        mass = mass_ref[l]
        ratio = jnp.full((1, LANES), LATENT, jnp.float32) / jnp.full((1, LANES), exner, jnp.float32)
        for h in range(2):
            cols = slice(h * LANES, (h + 1) * LANES)
            theta, vapor = thetas[h], vapors[h]
            cloud = cloud_ref[l, :, cols]
            temper = theta * exner
            saturation = scale * jnp.exp(temper)
            condensed = (vapor - saturation) / (1.0 + LATENT * saturation)
            saturation = scale * jnp.exp(temper + LATENT * condensed)
            condensed = condensed + (vapor - condensed - saturation) / (1.0 + LATENT * saturation)
            condensed = jnp.maximum(condensed, -cloud)
            theta_out[k, :, cols] = theta + condensed * ratio
            vapor_out[k, :, cols] = vapor - condensed
            liquid = cloud + condensed
            rained = AUTO_RATE * jnp.maximum(liquid - QCRIT, 0.0)
            cloud_out[k, :, cols] = liquid - rained
            rain_ref[:, cols] += mass * rained

    count = jnp.minimum(BLOCK_LEVELS, levels - step * BLOCK_LEVELS)
    unroll = WET_UNROLL if wet else DRY_UNROLL

    def sweep(start, stop, width):
        def body(m, carry):
            for j in range(width):
                (moist if wet else dry)(m * width + j)
            return carry

        lax.fori_loop(start, stop, body, 0)

    full = lax.div(count, unroll)
    sweep(0, full, unroll)
    if unroll > 2:
        sweep(full * (unroll // 2), lax.div(count, 2), 2)

    if not wet:
        return

    @pl.when(step == steps - 1)
    def _():
        for r in range(16):
            value = rain_ref[r : r + 1, :]
            coarse = value.astype(jnp.bfloat16)
            fine = (value - coarse.astype(jnp.float32)).astype(jnp.bfloat16)
            cols = slice(r * 256, (r + 1) * 256)
            here = onehot_ref[high:, cols]
            lo_ref[:LANES, cols] = here * coarse
            lo_ref[LANES:, cols] = here * fine
        placed = lax.dot_general(
            onehot_ref[:high, :],
            lo_ref[...],
            (((1,), (1,)), ((), ())),
            preferred_element_type=jnp.float32,
        )
        send_out[...] = placed[:, :LANES] + placed[:, LANES:]


SMEM = pl.BlockSpec(memory_space=pltpu.SMEM)
VMEM = pl.BlockSpec(memory_space=pltpu.VMEM)


def whole(a):
    return pl.BlockSpec(a.shape, lambda s: (0,) * len(a.shape))


def update(peers, wet, scalars, fields, marks, geometry, halos):
    levels = fields[0].shape[0]
    high = peers * 32
    block = pl.BlockSpec((BLOCK_LEVELS, 16, 256), lambda s: (s, 0, 0))
    field = jax.ShapeDtypeStruct(fields[0].shape, jnp.float32)
    sent = jax.ShapeDtypeStruct((high, LANES), jnp.float32)
    scratch = [
        pltpu.VMEM((7, 24, 256), jnp.float32),
        pltpu.VMEM((3, 24, LANES), jnp.float32),
        pltpu.VMEM((3, 24, LANES), jnp.float32),
    ]
    out_shape = [field] * len(fields)
    out_specs = [block] * len(fields)
    if wet:
        out_shape.append(sent)
        out_specs.append(whole(sent))
        scratch.append(pltpu.VMEM((16, 256), jnp.float32))
        scratch.append(pltpu.VMEM((2 * LANES, 4096), jnp.bfloat16))
    return pl.pallas_call(
        functools.partial(main_kernel, peers, levels, wet),
        grid=(pl.cdiv(levels, BLOCK_LEVELS),),
        in_specs=[SMEM] * len(scalars)
        + [VMEM] * (len(fields) + len(marks) + len(geometry) + len(halos)),
        out_specs=out_specs,
        out_shape=out_shape,
        scratch_shapes=scratch,
        name="moist" if wet else "dry",
        compiler_params=pltpu.CompilerParams(vmem_limit_bytes=32 * 2**20),
        cost_estimate=pl.CostEstimate(
            flops=10**8 * len(fields), transcendentals=0, bytes_accessed=2 * 2**20 * len(fields)
        ),
    )(*scalars, *fields, *marks, *geometry, *halos)


def on_device(
    theta,
    vapor,
    cloud,
    divergence,
    edge_weight,
    inv_area,
    damping,
    exner,
    sat_scale,
    layer_mass,
    span_of,
):
    peers = lax.axis_size("py")

    def fetch(x, axis, step):
        count = lax.axis_size(axis)
        return lax.ppermute(x, axis, [((i + step) % count, i) for i in range(count)])

    flat = lambda x: x.reshape(-1, 256)
    edge = flat(edge_weight)
    top, bot, left, right = pack(
        *(
            pltpu.with_memory_space_constraint(flat(x), pltpu.HBM)
            for x in (theta, vapor, divergence, edge_weight, inv_area)
        )
    )
    colr = fetch(left, "py", 1)
    coll = fetch(right, "py", -1)
    below = fetch(top, "px", 1)
    above = fetch(bot, "px", -1)
    marks = pltpu.with_memory_space_constraint(onehot(span_of, peers * 32), pltpu.VMEM)
    colr, coll, marks = lax.optimization_barrier((colr, coll, marks))
    sides = jnp.concatenate([colr, coll], axis=1)
    corner_below = fetch(sides[:8], "px", 1)
    corner_above = fetch(sides[8:], "px", -1)
    halos = tuple(
        pltpu.with_memory_space_constraint(x, pltpu.VMEM)
        for x in (below, above, colr, coll, corner_below, corner_above)
    )
    near = lambda x: pltpu.with_memory_space_constraint(x, pltpu.VMEM)
    halos = halos[:4] + (near(left), near(right)) + halos[4:]
    geometry = (near(edge), near(inv_area))
    theta_next, vapor_next, cloud_next, send = update(
        peers,
        True,
        (damping, exner, sat_scale, layer_mass),
        (near(theta), near(vapor), near(cloud)),
        (marks,),
        geometry,
        halos,
    )
    got = lax.all_to_all(send.reshape(peers, 32, LANES), "py", split_axis=0, concat_axis=0, tiled=True)
    (divergence_next,) = update(
        peers, False, (damping,), (near(divergence),), (), geometry, halos
    )
    precip = jnp.sum(got, axis=0).reshape(1, 4096)
    return (theta_next, vapor_next, cloud_next, divergence_next, precip)


def solution(mesh):
    field = P(None, "px", "py")
    plane = P("px", "py")
    return jax.shard_map(
        on_device,
        mesh=mesh,
        in_specs=(field, field, field, field, field, plane, P(), P(), P(), P(), plane),
        out_specs=(field, field, field, field, plane),
        check_vma=False,
    )
```

```python
import functools

import jax
import jax.numpy as jnp
from jax import lax
from jax.experimental import pallas as pl
from jax.experimental.pallas import tpu as pltpu
from jax.sharding import PartitionSpec as P

LATENT = 0.5
QCRIT = 0.2
AUTO_RATE = 0.5

LANES = 128
BLOCK_LEVELS = 32
WET_UNROLL = 4
DRY_UNROLL = 4


def pack_kernel(
    theta_hbm, vapor_hbm, div_hbm, edge_hbm, inv_hbm,
    top_ref, bot_ref, left_ref, right_ref,
    theta0, theta1, vapor0, vapor1, div0, div1, edge_ref, inv_ref, sems,
):
    levels = theta0.shape[0] // 16
    total = 3 * levels + 4
    fields = ((theta0, theta1), (vapor0, vapor1), (div0, div1))
    copies = []
    for field, source in enumerate((theta_hbm, vapor_hbm, div_hbm)):
        for half, ref in enumerate(fields[field]):
            part = source.at[:, half * LANES : (half + 1) * LANES]
            copies.append(pltpu.make_async_copy(part, ref, sems.at[2 * field + half]))
    geometry = [
        pltpu.make_async_copy(edge_hbm, edge_ref, sems.at[6]),
        pltpu.make_async_copy(inv_hbm, inv_ref, sems.at[7]),
    ]
    for copy in geometry + copies:
        copy.start()
    for copy in geometry:
        copy.wait()
    for out_ref, first in ((top_ref, 0), (bot_ref, 14)):
        for row in range(2):
            for g in range(3):
                out_ref[pl.ds(row * total + 3 * levels + g, 1), :] = edge_ref[
                    pl.ds(16 * g + first + row, 1), :
                ]
            out_ref[pl.ds(row * total + 3 * levels + 3, 1), :] = inv_ref[pl.ds(first + row, 1), :]
    pair = lax.broadcasted_iota(jnp.int32, (16, LANES), 1) >> 1
    low_base = 2 * total + 4

    def place(acc, value, slot, side):
        moved = pltpu.roll(value, (2 * slot + 2 * side) % LANES, 1)
        return jnp.where(pair == slot, moved, acc)

    for field, halves in enumerate(fields):
        for side in range(2):
            copies[2 * field + side].wait()
            cols = slice(side * LANES, (side + 1) * LANES)
            for out_ref, first in ((top_ref, 0), (bot_ref, 14)):
                for row in range(2):
                    out_ref[pl.ds(row * total + field * levels, levels), cols] = halves[side][
                        pl.ds(first + row, levels, stride=16), :
                    ]
            acc = jnp.zeros((16, LANES), jnp.float32)
            for l in range(levels):
                acc = place(acc, halves[side][16 * l : 16 * l + 16, :], l, side)
            if field == 0:
                cols = slice(side * LANES, (side + 1) * LANES)
                for g in range(4):
                    value = edge_ref[16 * g : 16 * g + 16, cols] if g < 3 else inv_ref[:, cols]
                    acc = place(acc, value, levels + g, side)
            cols = slice(field * LANES, (field + 1) * LANES)
            whole = left_ref if side == 0 else right_ref
            whole[:, cols] = acc
            slot = 3 * side + field
            rows = pl.ds(low_base + 8 * (slot // 2), 8)
            cols = slice((slot % 2) * LANES, (slot % 2 + 1) * LANES)
            top_ref[rows, cols] = acc[:8]
            bot_ref[rows, cols] = acc[8:]


def pack(theta, vapor, divergence, edge, inv):
    levels = theta.shape[0] // 16
    total = 3 * levels + 4
    rows = jax.ShapeDtypeStruct((2 * total + 28, 256), jnp.float32)
    cols = jax.ShapeDtypeStruct((16, 3 * LANES), jnp.float32)
    outs = (rows, rows, cols, cols)
    vmem = pl.BlockSpec(memory_space=pltpu.VMEM)
    return pl.pallas_call(
        pack_kernel,
        in_specs=[pl.BlockSpec(memory_space=pltpu.HBM)] * 5,
        out_specs=[vmem] * 4,
        out_shape=outs,
        scratch_shapes=[pltpu.VMEM((16 * levels, LANES), jnp.float32)] * 6
        + [
            pltpu.VMEM(edge.shape, jnp.float32),
            pltpu.VMEM(inv.shape, jnp.float32),
            pltpu.SemaphoreType.DMA((8,)),
        ],
        name="pack",
        compiler_params=pltpu.CompilerParams(vmem_limit_bytes=32 * 2**20),
    )(theta, vapor, divergence, edge, inv)


def onehot_kernel(high, span_ref, out_ref):
    def count(rows, shift):
        index = lax.broadcasted_iota(jnp.int32, (rows, 256), 0) - shift
        return index.astype(jnp.float32).astype(jnp.bfloat16)

    tall = count(high, high // 2)
    short = count(LANES, 0)
    one = jnp.bfloat16(1.0)
    zero = jnp.bfloat16(0.0)
    for r in range(span_ref.shape[0]):
        span = span_ref[r : r + 1, :]
        hi = ((span >> 7) - high // 2).astype(jnp.float32).astype(jnp.bfloat16)
        lo = (span & 127).astype(jnp.float32).astype(jnp.bfloat16)
        cols = slice(r * 256, (r + 1) * 256)
        out_ref[:high, cols] = jnp.where(tall == hi, one, zero)
        out_ref[high:, cols] = jnp.where(short == lo, one, zero)


def onehot(span, high):
    shape = jax.ShapeDtypeStruct((high + LANES, 4096), jnp.bfloat16)
    return pl.pallas_call(
        functools.partial(onehot_kernel, high),
        grid=(2,),
        in_specs=[pl.BlockSpec((8, 256), lambda s: (s, 0))],
        out_specs=pl.BlockSpec((high + LANES, 2048), lambda s: (0, s)),
        out_shape=shape,
        name="onehot",
        compiler_params=pltpu.CompilerParams(vmem_limit_bytes=32 * 2**20),
        cost_estimate=pl.CostEstimate(flops=10**9, transcendentals=0, bytes_accessed=5 * 2**20),
    )(span)


def up(v):
    return pltpu.roll(v, v.shape[0] - 1, 0)


def down(v):
    return pltpu.roll(v, 1, 0)


def ahead(v):
    return pltpu.roll(v, v.shape[1] - 1, 1)


def behind(v):
    return pltpu.roll(v, 1, 1)


def main_kernel(peers, levels, wet, *refs):
    total = 3 * levels + 4
    high = peers * 32
    step = pl.program_id(0)
    steps = pl.num_programs(0)
    if wet:
        damping_ref, exner_ref, scale_ref, mass_ref, theta_ref, vapor_ref, cloud_ref = refs[:7]
        onehot_ref = refs[7]
        theta_out, vapor_out, cloud_out, send_out = refs[18:22]
        coef_ref, edge_a, edge_b, rain_ref, lo_ref = refs[22:]
        halo_refs = refs[8:18]
    else:
        damping_ref, div_ref = refs[:2]
        halo_refs = refs[2:12]
        div_out, coef_ref, edge_a, edge_b = refs[12:]
    edge_ref, inv_ref, below_ref, above_ref, colr_ref, coll_ref = halo_refs[:6]
    ownl_ref, ownr_ref, corner_below, corner_above = halo_refs[6:]
    kinds = (0, 1) if wet else (2,)

    sub = lax.broadcasted_iota(jnp.int32, (8, 256), 0)
    sub_half = sub[:, :LANES]

    def row_tile(index):
        def row(ref, r):
            return jnp.broadcast_to(ref[pl.ds(r * total + index, 1), :], (8, 256))

        low = jnp.where(sub < 1, row(below_ref, 0), row(below_ref, 1))
        top = jnp.where(sub < 7, row(above_ref, 0), row(above_ref, 1))
        tile = jnp.where(sub < 4, low, top)
        return tile[:, :LANES], tile[:, LANES:]

    @pl.when(step == 0)
    def _():
        lane24 = lax.broadcasted_iota(jnp.int32, (24, LANES), 1)
        even = (lane24 & 1) == 0

        def packed(own, low, top, cols):
            corner = jnp.where(sub_half < 4, low, top)
            return jnp.concatenate([own[:, cols], corner], axis=0)

        def side_packs(field):
            cols = slice(field * LANES, (field + 1) * LANES)

            def inner(ref, slot):
                rows = pl.ds(2 * total + 4 + 8 * (slot // 2), 8)
                return ref[rows, (slot % 2) * LANES : (slot % 2 + 1) * LANES]

            far = slice((3 + field) * LANES, (4 + field) * LANES)
            v_r = packed(colr_ref, corner_below[:, cols], corner_above[:, cols], cols)
            v_l = packed(coll_ref, corner_below[:, far], corner_above[:, far], cols)
            o_l = packed(ownl_ref, inner(below_ref, field), inner(above_ref, field), cols)
            o_r = packed(ownr_ref, inner(below_ref, 3 + field), inner(above_ref, 3 + field), cols)
            return v_r, v_l, o_l, o_r

        packs = {field: side_packs(field) for field in {0, *kinds}}
        geo = []
        for g in range(4):
            slot = levels + g
            right = pltpu.roll(packs[0][0], (LANES - 2 * slot) % LANES, 1)
            left = pltpu.roll(packs[0][1], (2 * LANES - 2 - 2 * slot) % LANES, 1)
            side = jnp.where(lane24 < 64, right, left)
            centre = edge_ref[16 * g : 16 * g + 16, :] if g < 3 else inv_ref[...]
            tiles = row_tile(3 * levels + g)
            halves = [
                jnp.concatenate([centre[:, h * LANES : (h + 1) * LANES], tiles[h]], axis=0)
                for h in range(2)
            ]
            geo.append(jnp.concatenate(halves + [side], axis=1))
        w0, w1, w2, inv = geo
        c1 = inv * w0
        c2 = inv * down(w0)
        c3 = inv * w1
        c4 = inv * behind(w1)
        c5 = inv * w2
        c6 = inv * behind(up(w2))
        c0 = c1 + c2 + c3 + c4 + c5 + c6
        shifted = (c0, c1, c2, behind(c3), ahead(c4), behind(c5), ahead(c6))
        for k, c in enumerate(shifted):
            coef_ref[k] = c[:, :256]
        if wet:
            rain_ref[...] = jnp.zeros_like(rain_ref)

        def pick(c, col):
            return jnp.broadcast_to(c[:, col : col + 1], (24, LANES))

        k0, k1, k2, k3, k4, k5, k6 = (
            jnp.where(even, pick(c, 256), pick(c, 383)) for c in (c0, c1, c2, c3, c4, c5, c6)
        )
        x3 = jnp.where(even, pick(c3, 255), pick(c4, 0))
        x5 = jnp.where(even, pick(c5, 255), 0.0)
        x6 = jnp.where(even, 0.0, pick(c6, 0))
        for field in kinds:
            v_r, v_l, o_l, o_r = packs[field]
            v = jnp.where(even, v_r, v_l)
            v_up = up(v)
            v_dn = down(v)
            edge_a[field] = x3 * v + x5 * v_dn + x6 * v_up
            nxt = jnp.where(even, ahead(v_r), behind(o_l))
            prv = jnp.where(even, ahead(o_r), behind(v_l))
            first = (k1 * v_up + k2 * v_dn - k0 * v) + (
                (k3 * nxt + k5 * down(nxt)) + (k4 * prv + k6 * up(prv))
            )
            edge_b[field] = x3 * first + x5 * down(first) + x6 * up(first)

    def lap(halves, edge, rows):
        lane = lax.broadcasted_iota(jnp.int32, (rows, LANES), 1)
        a, b, c = [], [], []
        for h in range(2):
            cols = slice(h * LANES, (h + 1) * LANES)
            v_up = up(halves[h])[:rows]
            v_dn = down(halves[h])[:rows]
            v = halves[h][:rows]
            a.append(ahead(coef_ref[3, :rows, cols] * v + coef_ref[5, :rows, cols] * v_dn))
            b.append(behind(coef_ref[4, :rows, cols] * v + coef_ref[6, :rows, cols] * v_up))
            c.append(
                coef_ref[1, :rows, cols] * v_up
                + coef_ref[2, :rows, cols] * v_dn
                - coef_ref[0, :rows, cols] * v
            )
        last = lane == LANES - 1
        zero = lane == 0
        left = (jnp.where(last, a[1], a[0]) + jnp.where(zero, edge, b[0])) + c[0]
        right = (jnp.where(last, edge, a[1]) + jnp.where(zero, b[0], b[1])) + c[1]
        return left, right

    def damp(ref, field, l):
        turn = lax.rem(2 * LANES - 1 - 2 * l, LANES)
        centre = [ref[l, :, h * LANES : (h + 1) * LANES] for h in range(2)]
        tiles = row_tile(field * levels + l)
        first = lap(
            [jnp.concatenate([centre[h], tiles[h]], axis=0) for h in range(2)],
            pltpu.roll(edge_a[field], turn, 1),
            24,
        )
        second = lap(first, pltpu.roll(edge_b[field, :16], turn, 1), 16)
        rate = damping_ref[field, l]
        return [centre[h] - rate * second[h] for h in range(2)]

    def dry(k):
        div = damp(div_ref, 2, step * BLOCK_LEVELS + k)
        for h in range(2):
            div_out[k, :, h * LANES : (h + 1) * LANES] = div[h]

    def moist(k):
        l = step * BLOCK_LEVELS + k
        thetas = damp(theta_ref, 0, l)
        vapors = damp(vapor_ref, 1, l)
        exner = exner_ref[l]
        scale = scale_ref[l]
        mass = mass_ref[l]
        ratio = jnp.full((1, LANES), LATENT, jnp.float32) / jnp.full((1, LANES), exner, jnp.float32)
        for h in range(2):
            cols = slice(h * LANES, (h + 1) * LANES)
            theta, vapor = thetas[h], vapors[h]
            cloud = cloud_ref[l, :, cols]
            temper = theta * exner
            saturation = scale * jnp.exp(temper)
            condensed = (vapor - saturation) / (1.0 + LATENT * saturation)
            saturation = scale * jnp.exp(temper + LATENT * condensed)
            condensed = condensed + (vapor - condensed - saturation) / (1.0 + LATENT * saturation)
            condensed = jnp.maximum(condensed, -cloud)
            theta_out[k, :, cols] = theta + condensed * ratio
            vapor_out[k, :, cols] = vapor - condensed
            liquid = cloud + condensed
            rained = AUTO_RATE * jnp.maximum(liquid - QCRIT, 0.0)
            cloud_out[k, :, cols] = liquid - rained
            rain_ref[:, cols] += mass * rained

    count = jnp.minimum(BLOCK_LEVELS, levels - step * BLOCK_LEVELS)
    unroll = WET_UNROLL if wet else DRY_UNROLL

    def sweep(start, stop, width):
        def body(m, carry):
            for j in range(width):
                (moist if wet else dry)(m * width + j)
            return carry

        lax.fori_loop(start, stop, body, 0)

    full = lax.div(count, unroll)
    sweep(0, full, unroll)
    if unroll > 2:
        sweep(full * (unroll // 2), lax.div(count, 2), 2)

    if not wet:
        return

    @pl.when(step == steps - 1)
    def _():
        for r in range(16):
            value = rain_ref[r : r + 1, :]
            coarse = value.astype(jnp.bfloat16)
            fine = (value - coarse.astype(jnp.float32)).astype(jnp.bfloat16)
            cols = slice(r * 256, (r + 1) * 256)
            here = onehot_ref[high:, cols]
            lo_ref[:LANES, cols] = here * coarse
            lo_ref[LANES:, cols] = here * fine
        placed = lax.dot_general(
            onehot_ref[:high, :],
            lo_ref[...],
            (((1,), (1,)), ((), ())),
            preferred_element_type=jnp.float32,
        )
        send_out[...] = placed[:, :LANES] + placed[:, LANES:]


SMEM = pl.BlockSpec(memory_space=pltpu.SMEM)
VMEM = pl.BlockSpec(memory_space=pltpu.VMEM)


def whole(a):
    return pl.BlockSpec(a.shape, lambda s: (0,) * len(a.shape))


def update(peers, wet, scalars, fields, marks, geometry, halos):
    levels = fields[0].shape[0]
    high = peers * 32
    block = pl.BlockSpec((BLOCK_LEVELS, 16, 256), lambda s: (s, 0, 0))
    field = jax.ShapeDtypeStruct(fields[0].shape, jnp.float32)
    sent = jax.ShapeDtypeStruct((high, LANES), jnp.float32)
    scratch = [
        pltpu.VMEM((7, 24, 256), jnp.float32),
        pltpu.VMEM((3, 24, LANES), jnp.float32),
        pltpu.VMEM((3, 24, LANES), jnp.float32),
    ]
    out_shape = [field] * len(fields)
    out_specs = [block] * len(fields)
    if wet:
        out_shape.append(sent)
        out_specs.append(whole(sent))
        scratch.append(pltpu.VMEM((16, 256), jnp.float32))
        scratch.append(pltpu.VMEM((2 * LANES, 4096), jnp.bfloat16))
    return pl.pallas_call(
        functools.partial(main_kernel, peers, levels, wet),
        grid=(pl.cdiv(levels, BLOCK_LEVELS),),
        in_specs=[SMEM] * len(scalars)
        + [VMEM] * (len(fields) + len(marks) + len(geometry) + len(halos)),
        out_specs=out_specs,
        out_shape=out_shape,
        scratch_shapes=scratch,
        name="moist" if wet else "dry",
        compiler_params=pltpu.CompilerParams(vmem_limit_bytes=32 * 2**20),
        cost_estimate=pl.CostEstimate(
            flops=10**8 * len(fields), transcendentals=0, bytes_accessed=2 * 2**20 * len(fields)
        ),
    )(*scalars, *fields, *marks, *geometry, *halos)


def on_device(
    theta,
    vapor,
    cloud,
    divergence,
    edge_weight,
    inv_area,
    damping,
    exner,
    sat_scale,
    layer_mass,
    span_of,
):
    peers = lax.axis_size("py")

    def fetch(x, axis, step):
        count = lax.axis_size(axis)
        return lax.ppermute(x, axis, [((i + step) % count, i) for i in range(count)])

    flat = lambda x: x.reshape(-1, 256)
    edge = flat(edge_weight)
    top, bot, left, right = pack(
        *(
            pltpu.with_memory_space_constraint(flat(x), pltpu.HBM)
            for x in (theta, vapor, divergence, edge_weight, inv_area)
        )
    )
    colr = fetch(left, "py", 1)
    coll = fetch(right, "py", -1)
    below = fetch(top, "px", 1)
    above = fetch(bot, "px", -1)
    marks = pltpu.with_memory_space_constraint(onehot(span_of, peers * 32), pltpu.VMEM)
    colr, coll, marks = lax.optimization_barrier((colr, coll, marks))
    sides = jnp.concatenate([colr, coll], axis=1)
    corner_below = fetch(sides[:8], "px", 1)
    corner_above = fetch(sides[8:], "px", -1)
    halos = tuple(
        pltpu.with_memory_space_constraint(x, pltpu.VMEM)
        for x in (below, above, colr, coll, corner_below, corner_above)
    )
    near = lambda x: pltpu.with_memory_space_constraint(x, pltpu.VMEM)
    halos = halos[:4] + (near(left), near(right)) + halos[4:]
    geometry = (near(edge), near(inv_area))
    theta_next, vapor_next, cloud_next, send = update(
        peers,
        True,
        (damping, exner, sat_scale, layer_mass),
        (near(theta), near(vapor), near(cloud)),
        (marks,),
        geometry,
        halos,
    )
    got = lax.all_to_all(send.reshape(peers, 32, LANES), "py", split_axis=0, concat_axis=0, tiled=True)
    (divergence_next,) = update(
        peers, False, (damping,), (near(divergence),), (), geometry, halos
    )
    precip = jnp.sum(got, axis=0).reshape(1, 4096)
    return (theta_next, vapor_next, cloud_next, divergence_next, precip)


def solution(mesh):
    field = P(None, "px", "py")
    plane = P("px", "py")
    return jax.shard_map(
        on_device,
        mesh=mesh,
        in_specs=(field, field, field, field, field, plane, P(), P(), P(), P(), plane),
        out_specs=(field, field, field, field, plane),
        check_vma=False,
    )
```

```python
import functools

import jax
import jax.numpy as jnp
from jax import lax
from jax.experimental import pallas as pl
from jax.experimental.pallas import tpu as pltpu
from jax.sharding import PartitionSpec as P

LATENT = 0.5
QCRIT = 0.2
AUTO_RATE = 0.5

LANES = 128
BLOCK_LEVELS = 32
WET_UNROLL = 4
DRY_UNROLL = 4


def pack_kernel(
    theta_hbm, vapor_hbm, div_hbm, edge_hbm, inv_hbm,
    top_ref, bot_ref, left_ref, right_ref,
    theta0, theta1, vapor0, vapor1, div0, div1, edge_ref, inv_ref, sems,
):
    levels = theta0.shape[0] // 16
    total = 3 * levels + 4
    fields = ((theta0, theta1), (vapor0, vapor1), (div0, div1))
    copies = []
    for field, source in enumerate((theta_hbm, vapor_hbm, div_hbm)):
        for half, ref in enumerate(fields[field]):
            part = source.at[:, half * LANES : (half + 1) * LANES]
            copies.append(pltpu.make_async_copy(part, ref, sems.at[2 * field + half]))
    geometry = [
        pltpu.make_async_copy(edge_hbm, edge_ref, sems.at[6]),
        pltpu.make_async_copy(inv_hbm, inv_ref, sems.at[7]),
    ]
    for copy in geometry + copies:
        copy.start()
    for copy in geometry:
        copy.wait()
    for out_ref, first in ((top_ref, 0), (bot_ref, 14)):
        for row in range(2):
            for g in range(3):
                out_ref[pl.ds(row * total + 3 * levels + g, 1), :] = edge_ref[
                    pl.ds(16 * g + first + row, 1), :
                ]
            out_ref[pl.ds(row * total + 3 * levels + 3, 1), :] = inv_ref[pl.ds(first + row, 1), :]
    pair = lax.broadcasted_iota(jnp.int32, (16, LANES), 1) >> 1
    low_base = 2 * total + 4

    def place(acc, value, slot, side):
        moved = pltpu.roll(value, (2 * slot + 2 * side) % LANES, 1)
        return jnp.where(pair == slot, moved, acc)

    for field, halves in enumerate(fields):
        for side in range(2):
            copies[2 * field + side].wait()
            cols = slice(side * LANES, (side + 1) * LANES)
            for out_ref, first in ((top_ref, 0), (bot_ref, 14)):
                for row in range(2):
                    out_ref[pl.ds(row * total + field * levels, levels), cols] = halves[side][
                        pl.ds(first + row, levels, stride=16), :
                    ]
            acc = jnp.zeros((16, LANES), jnp.float32)
            for l in range(levels):
                acc = place(acc, halves[side][16 * l : 16 * l + 16, :], l, side)
            if field == 0:
                cols = slice(side * LANES, (side + 1) * LANES)
                for g in range(4):
                    value = edge_ref[16 * g : 16 * g + 16, cols] if g < 3 else inv_ref[:, cols]
                    acc = place(acc, value, levels + g, side)
            cols = slice(field * LANES, (field + 1) * LANES)
            whole = left_ref if side == 0 else right_ref
            whole[:, cols] = acc
            slot = 3 * side + field
            rows = pl.ds(low_base + 8 * (slot // 2), 8)
            cols = slice((slot % 2) * LANES, (slot % 2 + 1) * LANES)
            top_ref[rows, cols] = acc[:8]
            bot_ref[rows, cols] = acc[8:]


def pack(theta, vapor, divergence, edge, inv):
    levels = theta.shape[0] // 16
    total = 3 * levels + 4
    rows = jax.ShapeDtypeStruct((2 * total + 28, 256), jnp.float32)
    cols = jax.ShapeDtypeStruct((16, 3 * LANES), jnp.float32)
    outs = (rows, rows, cols, cols)
    vmem = pl.BlockSpec(memory_space=pltpu.VMEM)
    return pl.pallas_call(
        pack_kernel,
        in_specs=[pl.BlockSpec(memory_space=pltpu.HBM)] * 5,
        out_specs=[vmem] * 4,
        out_shape=outs,
        scratch_shapes=[pltpu.VMEM((16 * levels, LANES), jnp.float32)] * 6
        + [
            pltpu.VMEM(edge.shape, jnp.float32),
            pltpu.VMEM(inv.shape, jnp.float32),
            pltpu.SemaphoreType.DMA((8,)),
        ],
        name="pack",
        compiler_params=pltpu.CompilerParams(vmem_limit_bytes=32 * 2**20),
    )(theta, vapor, divergence, edge, inv)


def onehot_kernel(high, span_ref, out_ref):
    def count(rows, shift):
        index = lax.broadcasted_iota(jnp.int32, (rows, 256), 0) - shift
        return index.astype(jnp.float32).astype(jnp.bfloat16)

    tall = count(high, high // 2)
    short = count(LANES, 0)
    one = jnp.bfloat16(1.0)
    zero = jnp.bfloat16(0.0)
    for r in range(span_ref.shape[0]):
        span = span_ref[r : r + 1, :]
        hi = ((span >> 7) - high // 2).astype(jnp.float32).astype(jnp.bfloat16)
        lo = (span & 127).astype(jnp.float32).astype(jnp.bfloat16)
        cols = slice(r * 256, (r + 1) * 256)
        out_ref[:high, cols] = jnp.where(tall == hi, one, zero)
        out_ref[high:, cols] = jnp.where(short == lo, one, zero)


def onehot(span, high):
    shape = jax.ShapeDtypeStruct((high + LANES, 4096), jnp.bfloat16)
    return pl.pallas_call(
        functools.partial(onehot_kernel, high),
        grid=(2,),
        in_specs=[pl.BlockSpec((8, 256), lambda s: (s, 0))],
        out_specs=pl.BlockSpec((high + LANES, 2048), lambda s: (0, s)),
        out_shape=shape,
        name="onehot",
        compiler_params=pltpu.CompilerParams(vmem_limit_bytes=32 * 2**20),
        cost_estimate=pl.CostEstimate(flops=10**9, transcendentals=0, bytes_accessed=5 * 2**20),
    )(span)


def up(v):
    return pltpu.roll(v, v.shape[0] - 1, 0)


def down(v):
    return pltpu.roll(v, 1, 0)


def ahead(v):
    return pltpu.roll(v, v.shape[1] - 1, 1)


def behind(v):
    return pltpu.roll(v, 1, 1)


def main_kernel(peers, levels, wet, *refs):
    total = 3 * levels + 4
    high = peers * 32
    step = pl.program_id(0)
    steps = pl.num_programs(0)
    if wet:
        damping_ref, exner_ref, scale_ref, mass_ref, theta_ref, vapor_ref, cloud_ref = refs[:7]
        onehot_ref = refs[7]
        theta_out, vapor_out, cloud_out, send_out = refs[18:22]
        coef_ref, edge_a, edge_b, rain_ref, lo_ref = refs[22:]
        halo_refs = refs[8:18]
    else:
        damping_ref, div_ref = refs[:2]
        halo_refs = refs[2:12]
        div_out, coef_ref, edge_a, edge_b = refs[12:]
    edge_ref, inv_ref, below_ref, above_ref, colr_ref, coll_ref = halo_refs[:6]
    ownl_ref, ownr_ref, corner_below, corner_above = halo_refs[6:]
    kinds = (0, 1) if wet else (2,)

    sub = lax.broadcasted_iota(jnp.int32, (8, 256), 0)
    sub_half = sub[:, :LANES]

    def row_tile(index):
        def row(ref, r):
            return jnp.broadcast_to(ref[pl.ds(r * total + index, 1), :], (8, 256))

        low = jnp.where(sub < 1, row(below_ref, 0), row(below_ref, 1))
        top = jnp.where(sub < 7, row(above_ref, 0), row(above_ref, 1))
        tile = jnp.where(sub < 4, low, top)
        return tile[:, :LANES], tile[:, LANES:]

    @pl.when(step == 0)
    def _():
        lane24 = lax.broadcasted_iota(jnp.int32, (24, LANES), 1)
        even = (lane24 & 1) == 0

        def packed(own, low, top, cols):
            corner = jnp.where(sub_half < 4, low, top)
            return jnp.concatenate([own[:, cols], corner], axis=0)

        def side_packs(field):
            cols = slice(field * LANES, (field + 1) * LANES)

            def inner(ref, slot):
                rows = pl.ds(2 * total + 4 + 8 * (slot // 2), 8)
                return ref[rows, (slot % 2) * LANES : (slot % 2 + 1) * LANES]

            far = slice((3 + field) * LANES, (4 + field) * LANES)
            v_r = packed(colr_ref, corner_below[:, cols], corner_above[:, cols], cols)
            v_l = packed(coll_ref, corner_below[:, far], corner_above[:, far], cols)
            o_l = packed(ownl_ref, inner(below_ref, field), inner(above_ref, field), cols)
            o_r = packed(ownr_ref, inner(below_ref, 3 + field), inner(above_ref, 3 + field), cols)
            return v_r, v_l, o_l, o_r

        packs = {field: side_packs(field) for field in {0, *kinds}}
        geo = []
        for g in range(4):
            slot = levels + g
            right = pltpu.roll(packs[0][0], (LANES - 2 * slot) % LANES, 1)
            left = pltpu.roll(packs[0][1], (2 * LANES - 2 - 2 * slot) % LANES, 1)
            side = jnp.where(lane24 < 64, right, left)
            centre = edge_ref[16 * g : 16 * g + 16, :] if g < 3 else inv_ref[...]
            tiles = row_tile(3 * levels + g)
            halves = [
                jnp.concatenate([centre[:, h * LANES : (h + 1) * LANES], tiles[h]], axis=0)
                for h in range(2)
            ]
            geo.append(jnp.concatenate(halves + [side], axis=1))
        w0, w1, w2, inv = geo
        c1 = inv * w0
        c2 = inv * down(w0)
        c3 = inv * w1
        c4 = inv * behind(w1)
        c5 = inv * w2
        c6 = inv * behind(up(w2))
        c0 = c1 + c2 + c3 + c4 + c5 + c6
        shifted = (c0, c1, c2, behind(c3), ahead(c4), behind(c5), ahead(c6))
        for k, c in enumerate(shifted):
            coef_ref[k] = c[:, :256]
        if wet:
            rain_ref[...] = jnp.zeros_like(rain_ref)

        def pick(c, col):
            return jnp.broadcast_to(c[:, col : col + 1], (24, LANES))

        k0, k1, k2, k3, k4, k5, k6 = (
            jnp.where(even, pick(c, 256), pick(c, 383)) for c in (c0, c1, c2, c3, c4, c5, c6)
        )
        x3 = jnp.where(even, pick(c3, 255), pick(c4, 0))
        x5 = jnp.where(even, pick(c5, 255), 0.0)
        x6 = jnp.where(even, 0.0, pick(c6, 0))
        for field in kinds:
            v_r, v_l, o_l, o_r = packs[field]
            v = jnp.where(even, v_r, v_l)
            v_up = up(v)
            v_dn = down(v)
            edge_a[field] = x3 * v + x5 * v_dn + x6 * v_up
            nxt = jnp.where(even, ahead(v_r), behind(o_l))
            prv = jnp.where(even, ahead(o_r), behind(v_l))
            first = (k1 * v_up + k2 * v_dn - k0 * v) + (
                (k3 * nxt + k5 * down(nxt)) + (k4 * prv + k6 * up(prv))
            )
            edge_b[field] = x3 * first + x5 * down(first) + x6 * up(first)

    def lap(halves, edge, rows):
        lane = lax.broadcasted_iota(jnp.int32, (rows, LANES), 1)
        a, b, c = [], [], []
        for h in range(2):
            cols = slice(h * LANES, (h + 1) * LANES)
            v_up = up(halves[h])[:rows]
            v_dn = down(halves[h])[:rows]
            v = halves[h][:rows]
            a.append(ahead(coef_ref[3, :rows, cols] * v + coef_ref[5, :rows, cols] * v_dn))
            b.append(behind(coef_ref[4, :rows, cols] * v + coef_ref[6, :rows, cols] * v_up))
            c.append(
                coef_ref[1, :rows, cols] * v_up
                + coef_ref[2, :rows, cols] * v_dn
                - coef_ref[0, :rows, cols] * v
            )
        last = lane == LANES - 1
        zero = lane == 0
        left = (jnp.where(last, a[1], a[0]) + jnp.where(zero, edge, b[0])) + c[0]
        right = (jnp.where(last, edge, a[1]) + jnp.where(zero, b[0], b[1])) + c[1]
        return left, right

    def damp(ref, field, l):
        turn = lax.rem(2 * LANES - 1 - 2 * l, LANES)
        centre = [ref[l, :, h * LANES : (h + 1) * LANES] for h in range(2)]
        tiles = row_tile(field * levels + l)
        first = lap(
            [jnp.concatenate([centre[h], tiles[h]], axis=0) for h in range(2)],
            pltpu.roll(edge_a[field], turn, 1),
            24,
        )
        second = lap(first, pltpu.roll(edge_b[field, :16], turn, 1), 16)
        rate = damping_ref[field, l]
        return [centre[h] - rate * second[h] for h in range(2)]

    def dry(k):
        div = damp(div_ref, 2, step * BLOCK_LEVELS + k)
        for h in range(2):
            div_out[k, :, h * LANES : (h + 1) * LANES] = div[h]

    def moist(k):
        l = step * BLOCK_LEVELS + k
        thetas = damp(theta_ref, 0, l)
        vapors = damp(vapor_ref, 1, l)
        exner = exner_ref[l]
        scale = scale_ref[l]
        mass = mass_ref[l]
        ratio = jnp.full((1, LANES), LATENT, jnp.float32) / jnp.full((1, LANES), exner, jnp.float32)
        for h in range(2):
            cols = slice(h * LANES, (h + 1) * LANES)
            theta, vapor = thetas[h], vapors[h]
            cloud = cloud_ref[l, :, cols]
            temper = theta * exner
            saturation = scale * jnp.exp(temper)
            condensed = (vapor - saturation) / (1.0 + LATENT * saturation)
            saturation = scale * jnp.exp(temper + LATENT * condensed)
            condensed = condensed + (vapor - condensed - saturation) / (1.0 + LATENT * saturation)
            condensed = jnp.maximum(condensed, -cloud)
            theta_out[k, :, cols] = theta + condensed * ratio
            vapor_out[k, :, cols] = vapor - condensed
            liquid = cloud + condensed
            rained = AUTO_RATE * jnp.maximum(liquid - QCRIT, 0.0)
            cloud_out[k, :, cols] = liquid - rained
            rain_ref[:, cols] += mass * rained

    count = jnp.minimum(BLOCK_LEVELS, levels - step * BLOCK_LEVELS)
    unroll = WET_UNROLL if wet else DRY_UNROLL

    def sweep(start, stop, width):
        def body(m, carry):
            for j in range(width):
                (moist if wet else dry)(m * width + j)
            return carry

        lax.fori_loop(start, stop, body, 0)

    full = lax.div(count, unroll)
    sweep(0, full, unroll)
    if unroll > 2:
        sweep(full * (unroll // 2), lax.div(count, 2), 2)

    if not wet:
        return

    @pl.when(step == steps - 1)
    def _():
        for r in range(16):
            value = rain_ref[r : r + 1, :]
            coarse = value.astype(jnp.bfloat16)
            fine = (value - coarse.astype(jnp.float32)).astype(jnp.bfloat16)
            cols = slice(r * 256, (r + 1) * 256)
            here = onehot_ref[high:, cols]
            lo_ref[:LANES, cols] = here * coarse
            lo_ref[LANES:, cols] = here * fine
        placed = lax.dot_general(
            onehot_ref[:high, :],
            lo_ref[...],
            (((1,), (1,)), ((), ())),
            preferred_element_type=jnp.float32,
        )
        send_out[...] = placed[:, :LANES] + placed[:, LANES:]


SMEM = pl.BlockSpec(memory_space=pltpu.SMEM)
VMEM = pl.BlockSpec(memory_space=pltpu.VMEM)


def whole(a):
    return pl.BlockSpec(a.shape, lambda s: (0,) * len(a.shape))


def update(peers, wet, scalars, fields, marks, geometry, halos):
    levels = fields[0].shape[0]
    high = peers * 32
    block = pl.BlockSpec((BLOCK_LEVELS, 16, 256), lambda s: (s, 0, 0))
    field = jax.ShapeDtypeStruct(fields[0].shape, jnp.float32)
    sent = jax.ShapeDtypeStruct((high, LANES), jnp.float32)
    scratch = [
        pltpu.VMEM((7, 24, 256), jnp.float32),
        pltpu.VMEM((3, 24, LANES), jnp.float32),
        pltpu.VMEM((3, 24, LANES), jnp.float32),
    ]
    out_shape = [field] * len(fields)
    out_specs = [block] * len(fields)
    if wet:
        out_shape.append(sent)
        out_specs.append(whole(sent))
        scratch.append(pltpu.VMEM((16, 256), jnp.float32))
        scratch.append(pltpu.VMEM((2 * LANES, 4096), jnp.bfloat16))
    return pl.pallas_call(
        functools.partial(main_kernel, peers, levels, wet),
        grid=(pl.cdiv(levels, BLOCK_LEVELS),),
        in_specs=[SMEM] * len(scalars)
        + [VMEM] * (len(fields) + len(marks) + len(geometry) + len(halos)),
        out_specs=out_specs,
        out_shape=out_shape,
        scratch_shapes=scratch,
        name="moist" if wet else "dry",
        compiler_params=pltpu.CompilerParams(vmem_limit_bytes=32 * 2**20),
        cost_estimate=pl.CostEstimate(
            flops=10**8 * len(fields), transcendentals=0, bytes_accessed=2 * 2**20 * len(fields)
        ),
    )(*scalars, *fields, *marks, *geometry, *halos)


def on_device(
    theta,
    vapor,
    cloud,
    divergence,
    edge_weight,
    inv_area,
    damping,
    exner,
    sat_scale,
    layer_mass,
    span_of,
):
    peers = lax.axis_size("py")

    def fetch(x, axis, step):
        count = lax.axis_size(axis)
        return lax.ppermute(x, axis, [((i + step) % count, i) for i in range(count)])

    flat = lambda x: x.reshape(-1, 256)
    edge = flat(edge_weight)
    top, bot, left, right = pack(
        *(
            pltpu.with_memory_space_constraint(flat(x), pltpu.HBM)
            for x in (theta, vapor, divergence, edge_weight, inv_area)
        )
    )
    colr = fetch(left, "py", 1)
    coll = fetch(right, "py", -1)
    below = fetch(top, "px", 1)
    above = fetch(bot, "px", -1)
    marks = pltpu.with_memory_space_constraint(onehot(span_of, peers * 32), pltpu.VMEM)
    sides = jnp.concatenate([colr, coll], axis=1)
    corner_below = fetch(sides[:8], "px", 1)
    corner_above = fetch(sides[8:], "px", -1)
    halos = tuple(
        pltpu.with_memory_space_constraint(x, pltpu.VMEM)
        for x in (below, above, colr, coll, corner_below, corner_above)
    )
    near = lambda x: pltpu.with_memory_space_constraint(x, pltpu.VMEM)
    halos = halos[:4] + (near(left), near(right)) + halos[4:]
    geometry = (near(edge), near(inv_area))
    theta_next, vapor_next, cloud_next, send = update(
        peers,
        True,
        (damping, exner, sat_scale, layer_mass),
        (near(theta), near(vapor), near(cloud)),
        (marks,),
        geometry,
        halos,
    )
    got = lax.all_to_all(send.reshape(peers, 32, LANES), "py", split_axis=0, concat_axis=0, tiled=True)
    (divergence_next,) = update(
        peers, False, (damping,), (near(divergence),), (), geometry, halos
    )
    precip = jnp.sum(got, axis=0).reshape(1, 4096)
    return (theta_next, vapor_next, cloud_next, divergence_next, precip)


def solution(mesh):
    field = P(None, "px", "py")
    plane = P("px", "py")
    return jax.shard_map(
        on_device,
        mesh=mesh,
        in_specs=(field, field, field, field, field, plane, P(), P(), P(), P(), plane),
        out_specs=(field, field, field, field, plane),
        check_vma=False,
    )
```
